32 devices in a mesh: groups: 2 (over x), blk: 16 (over z, y, core).
Axes of the slice: x: 2, y: 2, z: 4, core: 2. Of those that a mesh axis runs over, the one named last changes fastest.
Arguments:
- queries: float32 [64, 8192], P(('groups', 'blk')), parts along dimension 0, may hold values from -50 to 50
- prefix_keys: float32 [4096, 512], P(('groups', 'blk')), parts along dimension 0, may hold values from -40 to 40
- prefix_values: float32 [4096, 512], P(('groups', 'blk')), parts along dimension 0, may hold values from -8 to 8
- out_weight: float32 [8192, 4096], P('blk'), may hold values from -0.0625 to 0.0625
- lengths: int32 [4], P('groups'), parts along dimension 0, may hold values from 512 to 2048, as said below
Outputs:
- mixed: float32 [64, 4096], P(('groups', 'blk')), parts along dimension 0
The draws below stay inside these ranges and needn't reach their ends.
There are 2 independent parts, one for each index of `groups`. The reference program is written for one: setup_inputs(seed, part) draws one part's arguments, and reference() takes and returns one part's arrays. A program takes and returns all parts, laid end to end along the dimension named above; an argument that names none is the same for every part. Nothing has to cross between parts.
Inputs may be any that keep to these rules, and one draw needn't show every extreme that they name: `lengths`: each request sees at least the first 512 prefix tokens, and some request sees all 2048 of them.
All inputs are finite; a program needn't handle non-finite values.
Results may differ from the reference program's by a relative error of at most 0.0003.
Values sent between devices are 32-bit elements; how exact they have to be, the bound alone decides.
No kernel may reach another device: no remote copies, remote signals or barrier semaphores. Data moves between devices by JAX's collectives and lax.ppermute only.
A program may use at most 128 MiB of HBM per device.

```python
import math
import jax
import jax.numpy as jnp
from jax import lax

D = 4096
H = 64
KVH = 4
HD = 128
REQ_TOK = 16
F = 8192
PREFIX = 2048
NEW = 32
REQUESTS = 2


def draw_queries(key, part):
    drawn_vals = jax.random.truncated_normal(jax.random.fold_in(key, 11), -4.0, 4.0, (NEW, H * HD))
    return drawn_vals.astype(jnp.float32)


def draw_prefix_keys(key, part):
    drawn_vals = 2.5 * jax.random.truncated_normal(jax.random.fold_in(key, 13), -4.0, 4.0, (PREFIX, KVH * HD))
    return drawn_vals.astype(jnp.float32)


def draw_lengths(key, part):
    keys_list = jax.random.split(jax.random.fold_in(key, 17), 2)
    drawn_vals = jax.random.randint(keys_list[0], (REQUESTS,), PREFIX // 4, PREFIX + 1)
    picked = jax.random.randint(keys_list[1], (), 0, REQUESTS)
    return jnp.where(jnp.arange(REQUESTS) == picked, PREFIX, drawn_vals).astype(jnp.int32)


def block_levels(key, shape, cuts, low, largest):
    factor_of, own = 1.0, jax.random.fold_in(key, 6)
    for axis_at, parts in cuts:
        steps = jnp.exp(jax.random.uniform(jax.random.fold_in(own, axis_at), (parts,), jnp.float32, low / len(cuts), largest / len(cuts)))
        factor_of = factor_of * jnp.repeat(steps, shape[axis_at] // parts).reshape([-1 if axis == axis_at else 1 for axis in range(len(shape))])
    return factor_of


def normal_values(rng, dims, width, bound, shards=(), kind=jnp.bfloat16):
    values = width * jax.random.normal(rng, dims, jnp.float32)
    if shards:
        values = values * block_levels(rng, dims, shards, -0.22, 0.18)
    return jnp.clip(values, -bound, bound).astype(kind)


def setup_inputs(seed: int = 0, part: int = 0) -> dict:
    streams_of = jax.random.split(jax.random.key(seed), 6)
    part_keys = jax.random.split(jax.random.fold_in(streams_of[5], part), 6)
    return {
        "queries": draw_queries(jax.random.fold_in(jax.random.fold_in(streams_of[5], part), 71), part),
        "prefix_keys": draw_prefix_keys(jax.random.fold_in(jax.random.fold_in(streams_of[5], part), 71), part),
        "prefix_values": normal_values(part_keys[2], (PREFIX, KVH * HD), 2.0, 8.0, ((0, 16),), jnp.float32),
        "out_weight": normal_values(streams_of[3], (F, D), F ** -0.5, 0.0625, ((0, 16),), jnp.float32),
        "lengths": draw_lengths(jax.random.fold_in(jax.random.fold_in(streams_of[5], part), 71), part),
    }


HIGHEST = lax.Precision.HIGHEST
NEG_FILL = -1e+30

def head_partials(query_rows, first_row, keys_split, values_split, key_pos, lengths):
    row_count = query_rows.shape[0]
    kv_count = keys_split.shape[1]
    head_count = query_rows.shape[1] // HD
    grouped = query_rows.reshape(row_count, kv_count, head_count // kv_count, HD)
    scores = jnp.einsum('tgje,pge->tgjp', grouped, keys_split, precision=HIGHEST, preferred_element_type=jnp.float32) * (1.0 / math.sqrt(HD))
    request_ids = (first_row + jnp.arange(row_count, dtype=jnp.int32)) // REQ_TOK
    request_table = jnp.arange(lengths.shape[0], dtype=jnp.int32)
    limits = lax.optimization_barrier(jnp.sum(jnp.where(request_ids[:, None] == request_table[None, :], lengths[None, :], 0), axis=1))
    visible = key_pos[None, :] < limits[:, None]
    visible_four = visible[:, None, None, :]
    masked = jnp.where(visible_four, scores, NEG_FILL)
    peak_vals = lax.optimization_barrier(jnp.max(masked, axis=3))
    weights = jnp.where(visible_four, jnp.exp(masked - peak_vals[..., None]), 0.0)
    totals = lax.optimization_barrier(jnp.sum(weights, axis=3))
    mixed_values = jnp.einsum('tgjp,pge->tgje', weights, values_split, precision=HIGHEST, preferred_element_type=jnp.float32)
    return (mixed_values.reshape(row_count, head_count * HD), peak_vals.reshape(row_count, head_count), totals.reshape(row_count, head_count))

def reference(queries, prefix_keys, prefix_values, out_weight, lengths):
    prefix_count = prefix_keys.shape[0]
    keys_split = prefix_keys.reshape(prefix_count, KVH, HD)
    values_split = prefix_values.reshape(prefix_count, KVH, HD)
    key_pos = jnp.arange(prefix_count, dtype=jnp.int32)
    request_blocks = queries.reshape(REQUESTS, REQ_TOK, H * HD)
    starts = jnp.arange(REQUESTS, dtype=jnp.int32) * REQ_TOK

    def attend(inputs):
        rows_now, first_row = inputs
        value_sums, peak_vals, weight_sums = head_partials(rows_now, first_row, keys_split, values_split, key_pos, lengths)
        return (value_sums.reshape(REQ_TOK, H, HD) / weight_sums[..., None]).reshape(REQ_TOK, H * HD)
    attended = lax.map(attend, (request_blocks, starts)).reshape(REQUESTS * REQ_TOK, H * HD)
    return jnp.dot(attended, out_weight, precision=HIGHEST, preferred_element_type=jnp.float32)
```

```python
import functools
import math

import jax
import jax.numpy as jnp
from jax import lax
from jax.experimental import pallas as pl
from jax.experimental.pallas import tpu as pltpu
from jax.sharding import PartitionSpec as P

H = 64
KVH = 4
HD = 128
REQ_TOK = 16
GROUP = H // KVH
LANES = 128

HIGHEST = lax.Precision.HIGHEST
NEG_FILL = -1e30


VMEM = pltpu.VMEM


def reverse_bits(value, bits):
    out = 0
    for b in range(bits):
        out |= ((value >> b) & 1) << (bits - 1 - b)
    return out


def swap_rows(x, size):
    blocks = [x[i * size : (i + 1) * size] for i in range(x.shape[0] // size)]
    return jnp.concatenate([blocks[i ^ 1] for i in range(len(blocks))], axis=0)


def lanes_of(columns, rows):
    lane = lax.broadcasted_iota(jnp.int32, (rows, LANES), 1)
    out = jnp.zeros((rows, LANES), jnp.float32)
    for i, column in enumerate(columns):
        out = jnp.where(lane == i, column, out)
    return out


def pack_kernel(sub, q_ref, k_ref, v_ref, *outs):
    plane = lax.axis_index("blk") // sub
    keys = k_ref.shape[0]
    for step in range(1, KVH):
        other = plane ^ step
        kv_out, q_out = outs[step - 1], outs[KVH - 1 + step - 1]
        lanes = pl.ds(pl.multiple_of(other * HD, HD), HD)
        kv_out[:keys, :] = k_ref[:, lanes]
        kv_out[keys:, :] = v_ref[:, lanes]
        wide = GROUP * HD
        q_out[...] = q_ref[:, pl.ds(pl.multiple_of(other * wide, wide), wide)]
    outs[-1][...] = q_ref[:, pl.ds(pl.multiple_of(plane * GROUP * HD, GROUP * HD), GROUP * HD)]


def pack(sub, queries, keys, values):
    kv = jax.ShapeDtypeStruct((2 * keys.shape[0], HD), jnp.float32)
    q = jax.ShapeDtypeStruct((queries.shape[0], GROUP * HD), jnp.float32)
    out = pl.pallas_call(
        functools.partial(pack_kernel, sub),
        out_shape=[kv] * (KVH - 1) + [q] * KVH,
        in_specs=[pl.BlockSpec(memory_space=VMEM)] * 3,
        out_specs=[pl.BlockSpec(memory_space=VMEM)] * (2 * KVH - 1),
        name="pack",
    )(queries, keys, values)
    return out[: KVH - 1], out[KVH - 1 : -1], out[-1]


def attend_kernel(bits, local_rows, key_count, len_ref, *refs):
    sub = 1 << bits
    q_refs, (k_ref, v_ref), pack_refs = refs[:sub], refs[sub : sub + 2], refs[sub + 2 : sub + 1 + KVH]
    send_ref, keep_ref = refs[sub + 1 + KVH :]
    position = lax.axis_index("blk")
    plane, place = position // sub, position % sub
    part = KVH * local_rows
    rows = part * sub
    per_owner = GROUP // sub

    lanes = pl.ds(pl.multiple_of(plane * HD, HD), HD)
    keys = jnp.concatenate([k_ref[:, lanes]] + [r[:key_count, :] for r in pack_refs], axis=0)
    values = jnp.concatenate([v_ref[:, lanes]] + [r[key_count:, :] for r in pack_refs], axis=0)
    held = key_count * KVH

    pieces = []
    for order in range(sub):
        owner = place ^ reverse_bits(order, bits)
        for i in range(per_owner):
            at = pl.ds(pl.multiple_of((owner * per_owner + i) * HD, HD), HD)
            pieces += [q_ref[:, at] for q_ref in q_refs]
    stacked = jnp.concatenate(pieces, axis=0)
    scores = lax.dot_general(
        stacked, keys, (((1,), (1,)), ((), ())), precision=HIGHEST, preferred_element_type=jnp.float32
    ) * (1.0 / math.sqrt(HD))
    scores = scores.reshape(GROUP, rows, held)

    row = lax.broadcasted_iota(jnp.int32, (rows, 1), 0)
    order = row // part
    within = row % part
    rel = (within // local_rows) * sub
    for b in range(bits):
        rel = rel + ((order >> (bits - 1 - b)) & 1) * (1 << b)
    token = (position ^ rel) * local_rows + within % local_rows
    request = token // REQ_TOK
    limits = jnp.zeros((rows, 1), jnp.int32)
    for i in range(len_ref.shape[0]):
        limits = jnp.where(request == i, len_ref[i], limits)
    at = lax.broadcasted_iota(jnp.int32, (1, held), 1)
    source = (plane ^ (at // key_count)) * sub + place
    visible = (source * key_count + at % key_count) < limits
    visible = jnp.broadcast_to(visible[None], scores.shape)

    masked = jnp.where(visible, scores, NEG_FILL)
    peaks = jnp.max(masked, axis=2, keepdims=True)
    weights = jnp.where(visible, jnp.exp(masked - peaks), 0.0)
    totals = jnp.sum(weights, axis=2, keepdims=True)
    sums = jnp.dot(
        weights.reshape(GROUP * rows, held), values, precision=HIGHEST, preferred_element_type=jnp.float32
    ).reshape(GROUP, rows, HD)

    half = GROUP // 2
    for start, ref in ((0, keep_ref), (half, send_ref)):
        for i in range(half):
            ref[:, i * HD : (i + 1) * HD] = sums[start + i]
        stats = [peaks[start + i] for i in range(half)] + [totals[start + i] for i in range(half)]
        ref[:, half * HD :] = lanes_of(stats, rows)


def attend(bits, local_rows, lengths, q_parts, keys, values, packs):
    sub = 1 << bits
    rows = KVH * local_rows * sub
    out = jax.ShapeDtypeStruct((rows, GROUP // 2 * HD + LANES), jnp.float32)
    return pl.pallas_call(
        functools.partial(attend_kernel, bits, local_rows, keys.shape[0]),
        out_shape=[out, out],
        in_specs=[pl.BlockSpec(memory_space=pltpu.SMEM)]
        + [pl.BlockSpec(memory_space=VMEM)] * (sub + 1 + KVH),
        out_specs=[pl.BlockSpec(memory_space=VMEM)] * 2,
        name="attend",
    )(lengths, *q_parts, keys, values, *packs)


def merged(keep_ref, recv_ref, swap):
    heads = (keep_ref.shape[1] - LANES) // HD
    mine, other = keep_ref[:, heads * HD :], swap_rows(recv_ref[:, heads * HD :], swap)
    sums, peaks, totals = [], [], []
    for i in range(heads):
        peak_a, peak_b = mine[:, i : i + 1], other[:, i : i + 1]
        peak = jnp.maximum(peak_a, peak_b)
        factor_a, factor_b = jnp.exp(peak_a - peak), jnp.exp(peak_b - peak)
        cols = slice(i * HD, (i + 1) * HD)
        sums.append(keep_ref[:, cols] * factor_a + swap_rows(recv_ref[:, cols], swap) * factor_b)
        peaks.append(peak)
        totals.append(
            mine[:, heads + i : heads + i + 1] * factor_a + other[:, heads + i : heads + i + 1] * factor_b
        )
    return sums, peaks, totals


def merge_kernel(swap, keep_ref, recv_ref, send_out, keep_out):
    sums, peaks, totals = merged(keep_ref, recv_ref, swap)
    half = len(sums) // 2
    for start, ref in ((0, keep_out), (half, send_out)):
        for i in range(half):
            ref[:, i * HD : (i + 1) * HD] = sums[start + i]
        stats = peaks[start : start + half] + totals[start : start + half]
        ref[:, half * HD :] = lanes_of(stats, keep_ref.shape[0])


def merge(swap, keep, recv):
    rows, width = keep.shape
    half = (width - LANES) // HD // 2
    out = jax.ShapeDtypeStruct((rows, half * HD + LANES), jnp.float32)
    return pl.pallas_call(
        functools.partial(merge_kernel, swap),
        out_shape=[out, out],
        in_specs=[pl.BlockSpec(memory_space=VMEM)] * 2,
        out_specs=[pl.BlockSpec(memory_space=VMEM)] * 2,
        name="merge",
    )(keep, recv)


def project_kernel(swap, tile, keep_ref, recv_ref, w_ref, send_out, keep_out, w_buf, sems):
    features, width = w_ref.shape
    chunks = width // tile
    copies = [
        pltpu.make_async_copy(w_ref.at[:, pl.ds(c * tile, tile)], w_buf.at[c], sems.at[c])
        for c in range(chunks)
    ]
    for copy in copies:
        copy.start()
    sums, _, totals = merged(keep_ref, recv_ref, swap)
    attended = jnp.concatenate([a / t for a, t in zip(sums, totals)], axis=1)
    half = attended.shape[0] // 2
    for c in range(chunks):
        copies[c].wait()
        out = jnp.dot(attended, w_buf[c], precision=HIGHEST, preferred_element_type=jnp.float32)
        cols = slice(c * tile, (c + 1) * tile)
        keep_out[:, cols] = out[:half]
        send_out[:, cols] = out[half:]


def project(swap, keep, recv, weight):
    features, width = weight.shape
    tile = min(width, 512)
    out = jax.ShapeDtypeStruct((keep.shape[0] // 2, width), jnp.float32)
    return pl.pallas_call(
        functools.partial(project_kernel, swap, tile),
        out_shape=[out, out],
        in_specs=[pl.BlockSpec(memory_space=VMEM)] * 2 + [pl.BlockSpec(memory_space=pl.ANY)],
        out_specs=[pl.BlockSpec(memory_space=VMEM)] * 2,
        scratch_shapes=[
            pltpu.VMEM((width // tile, features, tile), jnp.float32),
            pltpu.SemaphoreType.DMA((width // tile,)),
        ],
        name="project",
    )(keep, recv, weight)


def by_planes(bits, queries, keys, values, weight, lengths):
    blocks = lax.axis_size("blk")
    sub = 1 << bits
    local_rows = queries.shape[0]
    part = KVH * local_rows

    def swap(x, mask):
        return lax.ppermute(x, "blk", [(i, i ^ mask) for i in range(blocks)])

    kv_send, q_send, q_own = pack(sub, queries, keys, values)
    q_rows = [q_own] + [swap(q_send[k - 1], k * sub) for k in range(1, KVH)]
    kv_held = [swap(kv_send[k - 1], k * sub) for k in range(1, KVH)]
    q_parts = [jnp.concatenate(q_rows, axis=0)]
    for b in reversed(range(bits)):
        q_parts = q_parts + [swap(x, 1 << b) for x in q_parts]

    send, keep = attend(bits, local_rows, lengths, q_parts, keys, values, kv_held)
    for b in range(bits - 1):
        send, keep = merge(part << (bits - 1 - b), keep, swap(send, 1 << b))
    send, keep = project(part, keep, swap(send, 1 << (bits - 1)), weight)

    total = keep + swap(send, 1)
    for b in range(1, bits):
        half = total.shape[0] // 2
        total = total[:half] + swap(total[half:], 1 << b)
    out = total[:local_rows]
    for k in range(1, KVH):
        out = out + swap(total[k * local_rows : (k + 1) * local_rows], k * sub)
    return out


def head_partials(query_rows, keys_held, values_held, key_pos, lengths):
    row_count = query_rows.shape[0]
    grouped = query_rows.reshape(row_count, GROUP, HD)
    scores = jnp.einsum(
        "tje,pe->tjp", grouped, keys_held, precision=HIGHEST, preferred_element_type=jnp.float32
    ) * (1.0 / math.sqrt(HD))
    request_ids = jnp.arange(row_count, dtype=jnp.int32) // REQ_TOK
    request_table = jnp.arange(lengths.shape[0], dtype=jnp.int32)
    limits = jnp.sum(
        jnp.where(request_ids[:, None] == request_table[None, :], lengths[None, :], 0), axis=1
    )
    visible = (key_pos[None, :] < limits[:, None])[:, None, :]
    masked = jnp.where(visible, scores, NEG_FILL)
    peak_vals = jnp.max(masked, axis=2)
    weights = jnp.where(visible, jnp.exp(masked - peak_vals[..., None]), 0.0)
    totals = jnp.sum(weights, axis=2)
    mixed_values = jnp.einsum(
        "tjp,pe->tje", weights, values_held, precision=HIGHEST, preferred_element_type=jnp.float32
    )
    return mixed_values.reshape(row_count, GROUP * HD), peak_vals, totals


def by_all_to_all(queries, keys, values, weight, lengths):
    blocks = lax.axis_size("blk")
    position = lax.axis_index("blk")
    local_rows = queries.shape[0]
    total_rows = local_rows * blocks
    key_count = keys.shape[0]
    sub_count = blocks // KVH
    sub_len = key_count // sub_count

    def exchange(x, split, concat):
        return lax.all_to_all(x, "blk", split_axis=split, concat_axis=concat, tiled=True)

    def spread(x):
        split = x.reshape(sub_count, sub_len, KVH, HD).transpose(0, 2, 1, 3)
        return exchange(split.reshape(blocks, sub_len, HD), 0, 0).reshape(blocks * sub_len, HD)

    held_pos = (
        jnp.arange(blocks, dtype=jnp.int32)[:, None] * key_count
        + position // KVH * sub_len
        + jnp.arange(sub_len, dtype=jnp.int32)[None, :]
    ).reshape(blocks * sub_len)
    query_heads = queries.reshape(local_rows, KVH, GROUP * HD).transpose(1, 0, 2)
    query_send = jnp.broadcast_to(query_heads[None], (sub_count, KVH, local_rows, GROUP * HD))
    query_held = exchange(query_send.reshape(blocks, local_rows, GROUP * HD), 0, 0)
    sums, peaks, totals = head_partials(
        query_held.reshape(total_rows, GROUP * HD), spread(keys), spread(values), held_pos, lengths
    )
    sums = exchange(sums, 0, 0).reshape(sub_count, KVH, local_rows, GROUP, HD)
    peaks = exchange(peaks, 0, 0).reshape(sub_count, KVH, local_rows, GROUP)
    totals = exchange(totals, 0, 0).reshape(sub_count, KVH, local_rows, GROUP)
    factor = jnp.exp(peaks - jnp.max(peaks, axis=0)[None])
    numerator = jnp.sum(sums * factor[..., None], axis=0)
    denominator = jnp.sum(totals * factor, axis=0)
    attended = (numerator / denominator[..., None]).transpose(1, 0, 2, 3).reshape(local_rows, H * HD)
    feature_rows = exchange(attended, 1, 0)
    parts = jnp.dot(feature_rows, weight, precision=HIGHEST, preferred_element_type=jnp.float32)
    return jnp.sum(exchange(parts, 0, 0).reshape(blocks, local_rows, weight.shape[1]), axis=0)


def per_device(queries, prefix_keys, prefix_values, out_weight, lengths):
    blocks = lax.axis_size("blk")
    sub = blocks // KVH
    bits = sub.bit_length() - 1
    fits = (
        blocks == KVH << bits
        and bits >= 1
        and GROUP % sub == 0
        and (KVH * queries.shape[0]) % 8 == 0
        and prefix_keys.shape[0] % LANES == 0
    )
    if fits:
        return by_planes(bits, queries, prefix_keys, prefix_values, out_weight, lengths)
    return by_all_to_all(queries, prefix_keys, prefix_values, out_weight, lengths)


def solution(mesh):
    in_specs = (
        P(("groups", "blk"), None),
        P(("groups", "blk"), None),
        P(("groups", "blk"), None),
        P("blk", None),
        P("groups"),
    )
    out_specs = P(("groups", "blk"), None)
    return jax.shard_map(
        per_device, mesh=mesh, in_specs=in_specs, out_specs=out_specs, check_vma=False
    )
```

```python
import functools
import math

import jax
import jax.numpy as jnp
from jax import lax
from jax.experimental import pallas as pl
from jax.experimental.pallas import tpu as pltpu
from jax.sharding import PartitionSpec as P


H = 64
KVH = 4
HD = 128
REQ_TOK = 16
GROUP = H // KVH
LANES = 128

HIGHEST = lax.Precision.HIGHEST
NEG_FILL = -1e30


VMEM = pltpu.VMEM


def reverse_bits(value, bits):
    out = 0
    for b in range(bits):
        out |= ((value >> b) & 1) << (bits - 1 - b)
    return out


def swap_rows(x, size):
    blocks = [x[i * size : (i + 1) * size] for i in range(x.shape[0] // size)]
    return jnp.concatenate([blocks[i ^ 1] for i in range(len(blocks))], axis=0)


def lanes_of(columns, rows):
    lane = lax.broadcasted_iota(jnp.int32, (rows, LANES), 1)
    out = jnp.zeros((rows, LANES), jnp.float32)
    for i, column in enumerate(columns):
        out = jnp.where(lane == i, column, out)
    return out


def pieces_of(x, count):
    out = []
    for _ in range(count):
        out.append(x.astype(jnp.bfloat16))
        x = x - out[-1].astype(jnp.float32)
    return out


def times(a, b, dims=(((1,), (0,)), ((), ()))):
    return lax.dot_general(a, b, dims, preferred_element_type=jnp.float32)


def limit(mib):
    return pltpu.CompilerParams(vmem_limit_bytes=mib << 20)


IN_VMEM = pl.BlockSpec(memory_space=VMEM)
IN_PLACE = pl.BlockSpec(memory_space=pl.ANY)


def in_hbm(x):
    return pltpu.with_memory_space_constraint(x, pltpu.HBM)


def pack_kernel(sub, q_hbm, k_hbm, v_hbm, *refs):
    outs, sems = refs[:-1], refs[-1]
    plane = lax.axis_index("blk") // sub
    keys, wide = k_hbm.shape[0], GROUP * HD
    copies = []
    for step in (2, 3, 1, 0) if KVH == 4 else range(KVH):
        other = plane ^ step
        lanes = pl.ds(pl.multiple_of(other * HD, HD), HD)
        q_lanes = pl.ds(pl.multiple_of(other * wide, wide), wide)
        copies += [
            (k_hbm.at[:, lanes], outs[step].at[pl.ds(0, keys), :]),
            (v_hbm.at[:, lanes], outs[step].at[pl.ds(keys, keys), :]),
            (q_hbm.at[:, q_lanes], outs[KVH + step]),
        ]
    copies = [pltpu.make_async_copy(src, dst, sems.at[i]) for i, (src, dst) in enumerate(copies)]
    for copy in copies:
        copy.start()
    for copy in copies:
        copy.wait()


def pack(sub, queries, keys, values):
    kv = jax.ShapeDtypeStruct((2 * keys.shape[0], HD), jnp.float32)
    q = jax.ShapeDtypeStruct((queries.shape[0], GROUP * HD), jnp.float32)
    out = pl.pallas_call(
        functools.partial(pack_kernel, sub),
        out_shape=[kv] * KVH + [q] * KVH,
        in_specs=[IN_PLACE] * 3,
        out_specs=[IN_VMEM] * (2 * KVH),
        scratch_shapes=[pltpu.SemaphoreType.DMA((3 * KVH,))],
        compiler_params=limit(4),
        name="pack",
    )(in_hbm(queries), in_hbm(keys), in_hbm(values))
    return out[:KVH], out[KVH:]


def split_kernel(tile, w_hbm, high_ref, low_ref, buf, sems):
    chunks = w_hbm.shape[0] // tile
    copies = [
        pltpu.make_async_copy(w_hbm.at[pl.ds(c * tile, tile), :], buf.at[c], sems.at[c])
        for c in range(chunks)
    ]
    for copy in copies:
        copy.start()
    for c in range(chunks):
        copies[c].wait()
        rows = slice(c * tile, (c + 1) * tile)
        high_ref[rows, :], low_ref[rows, :] = pieces_of(buf[c], 2)


def split_weight(weight):
    features, width = weight.shape
    tile = min(features, 64)
    out = jax.ShapeDtypeStruct((features, width), jnp.bfloat16)
    return pl.pallas_call(
        functools.partial(split_kernel, tile),
        out_shape=[out, out],
        in_specs=[IN_PLACE],
        out_specs=[IN_VMEM] * 2,
        scratch_shapes=[
            pltpu.VMEM((features // tile, tile, width), jnp.float32),
            pltpu.SemaphoreType.DMA((features // tile,)),
        ],
        compiler_params=limit(20),
        cost_estimate=pl.CostEstimate(
            flops=8 * features * width, bytes_accessed=8 * features * width, transcendentals=0
        ),
        name="split",
    )(in_hbm(weight))


def attend_kernel(bits, local_rows, key_count, len_ref, *refs):
    sub = 1 << bits
    q_refs, kv_refs = refs[:sub], refs[sub : sub + KVH]
    send_ref, keep_ref = refs[sub + KVH :]
    position = lax.axis_index("blk")
    plane, place = position // sub, position % sub
    part = KVH * local_rows
    rows = part * sub
    per_owner = GROUP // sub
    held = key_count * KVH

    row = lax.broadcasted_iota(jnp.int32, (rows, 1), 0)
    order = row // part
    within = row % part
    rel = (within // local_rows) * sub
    for b in range(bits):
        rel = rel + ((order >> (bits - 1 - b)) & 1) * (1 << b)
    token = (position ^ rel) * local_rows + within % local_rows
    request = token // REQ_TOK
    limits = jnp.zeros((rows, 1), jnp.int32)
    for i in range(len_ref.shape[0]):
        limits = jnp.where(request == i, len_ref[i], limits)
    at = lax.broadcasted_iota(jnp.int32, (1, held), 1)
    source = (plane ^ (at // key_count)) * sub + place
    visible = (source * key_count + at % key_count) < limits

    keys = jnp.concatenate([r[:key_count, :] for r in kv_refs], axis=0)
    values = jnp.concatenate([r[key_count:, :] for r in kv_refs], axis=0)
    k1, k2, k3 = pieces_of(keys, 3)
    k12, k31 = jnp.concatenate([k1, k2], axis=1), jnp.concatenate([k3, k1], axis=1)
    v1, v2 = pieces_of(values, 2)
    v12 = jnp.concatenate([v1, v2], axis=1)
    both = (((1,), (1,)), ((), ()))
    scale = 1.0 / math.sqrt(HD)

    half = GROUP // 2
    for ref, start in ((send_ref, half), (keep_ref, 0)):
        peaks, totals = [], []
        for i in range(half):
            head = start + i
            owner = place ^ reverse_bits(head // per_owner, bits)
            lanes = pl.ds(pl.multiple_of((owner * per_owner + head % per_owner) * HD, HD), HD)
            q = jnp.concatenate([q_ref[:, lanes] for q_ref in q_refs], axis=0)
            q1, q2, q3 = pieces_of(q, 3)
            q11, q22 = jnp.concatenate([q1, q1], axis=1), jnp.concatenate([q2, q2], axis=1)
            q13 = jnp.concatenate([q1, q3], axis=1)
            top = times(jnp.concatenate([q11, q22], axis=0), k12, both)
            scores = (top[:rows] + (top[rows:] + times(q13, k31, both))) * scale
            masked = jnp.where(visible, scores, NEG_FILL)
            peak = jnp.max(masked, axis=1, keepdims=True)
            weights = jnp.where(visible, jnp.exp(masked - peak), 0.0)
            w1, w2 = pieces_of(weights, 2)
            wide = times(w1, v12)
            ref[:, i * HD : (i + 1) * HD] = wide[:, :HD] + (wide[:, HD:] + times(w2, v1))
            peaks.append(peak)
            totals.append(jnp.sum(weights, axis=1, keepdims=True))
        ref[:, half * HD :] = lanes_of(peaks + totals, rows)


def attend(bits, local_rows, lengths, q_parts, kv_held):
    sub = 1 << bits
    rows = KVH * local_rows * sub
    out = jax.ShapeDtypeStruct((rows, GROUP // 2 * HD + LANES), jnp.float32)
    return pl.pallas_call(
        functools.partial(attend_kernel, bits, local_rows, kv_held[0].shape[0] // 2),
        out_shape=[out, out],
        in_specs=[pl.BlockSpec(memory_space=pltpu.SMEM)] + [IN_VMEM] * (sub + KVH),
        out_specs=[IN_VMEM] * 2,
        compiler_params=limit(16),
        name="attend",
    )(lengths, *q_parts, *kv_held)


def merged(keep_ref, recv_ref, swap):
    heads = (keep_ref.shape[1] - LANES) // HD
    mine, other = keep_ref[:, heads * HD :], swap_rows(recv_ref[:, heads * HD :], swap)
    sums, peaks, totals = [], [], []
    for i in range(heads):
        peak_a, peak_b = mine[:, i : i + 1], other[:, i : i + 1]
        peak = jnp.maximum(peak_a, peak_b)
        factor_a, factor_b = jnp.exp(peak_a - peak), jnp.exp(peak_b - peak)
        cols = slice(i * HD, (i + 1) * HD)
        sums.append(keep_ref[:, cols] * factor_a + swap_rows(recv_ref[:, cols], swap) * factor_b)
        peaks.append(peak)
        totals.append(
            mine[:, heads + i : heads + i + 1] * factor_a + other[:, heads + i : heads + i + 1] * factor_b
        )
    return sums, peaks, totals


def merge_kernel(swap, keep_ref, recv_ref, send_out, keep_out):
    sums, peaks, totals = merged(keep_ref, recv_ref, swap)
    half = len(sums) // 2
    for start, ref in ((0, keep_out), (half, send_out)):
        for i in range(half):
            ref[:, i * HD : (i + 1) * HD] = sums[start + i]
        stats = peaks[start : start + half] + totals[start : start + half]
        ref[:, half * HD :] = lanes_of(stats, keep_ref.shape[0])


def merge(swap, keep, recv):
    rows, width = keep.shape
    half = (width - LANES) // HD // 2
    out = jax.ShapeDtypeStruct((rows, half * HD + LANES), jnp.float32)
    return pl.pallas_call(
        functools.partial(merge_kernel, swap),
        out_shape=[out, out],
        in_specs=[IN_VMEM] * 2,
        out_specs=[IN_VMEM] * 2,
        compiler_params=limit(4),
        name="merge",
    )(keep, recv)


def project_kernel(swap, tile, keep_ref, recv_ref, high_ref, low_ref, send_out, keep_out):
    sums, _, totals = merged(keep_ref, recv_ref, swap)
    attended = jnp.concatenate([a / t for a, t in zip(sums, totals)], axis=1)
    rows = attended.shape[0]
    half = rows // 2
    a1, a2 = pieces_of(attended, 2)
    a12 = jnp.concatenate([a1, a2], axis=0)
    for c in range(high_ref.shape[1] // tile):
        cols = slice(c * tile, (c + 1) * tile)
        top = times(a12, high_ref[:, cols])
        out = top[:rows] + (top[rows:] + times(a1, low_ref[:, cols]))
        keep_out[:, cols] = out[:half]
        send_out[:, cols] = out[half:]


def project(swap, keep, recv, high, low):
    width = high.shape[1]
    out = jax.ShapeDtypeStruct((keep.shape[0] // 2, width), jnp.float32)
    return pl.pallas_call(
        functools.partial(project_kernel, swap, min(width, 512)),
        out_shape=[out, out],
        in_specs=[IN_VMEM] * 4,
        out_specs=[IN_VMEM] * 2,
        compiler_params=limit(16),
        name="project",
    )(keep, recv, high, low)


def by_planes(bits, queries, keys, values, weight, lengths):
    blocks = lax.axis_size("blk")
    sub = 1 << bits
    local_rows = queries.shape[0]
    part = KVH * local_rows

    def swap(x, mask):
        return lax.ppermute(x, "blk", [(i, i ^ mask) for i in range(blocks)])

    kv_send, q_send = pack(sub, queries, keys, values)
    kv_held = [kv_send[0]] + [swap(kv_send[k], k * sub) for k in range(1, KVH)]
    q_rows = [q_send[0]] + [swap(q_send[k], k * sub) for k in range(1, KVH)]
    q_parts = [jnp.concatenate(q_rows, axis=0)]
    for b in reversed(range(bits)):
        q_parts = q_parts + [swap(x, 1 << b) for x in q_parts]
    high, low = split_weight(weight)

    send, keep = attend(bits, local_rows, lengths, q_parts, kv_held)
    for b in range(bits - 1):
        send, keep = merge(part << (bits - 1 - b), keep, swap(send, 1 << b))
    send, keep = project(part, keep, swap(send, 1 << (bits - 1)), high, low)

    recv = swap(send, 1)
    for b in range(1, bits):
        half = keep.shape[0] // 2
        send = keep[half:] + recv[half:]
        keep = keep[:half] + recv[:half]
        recv = swap(send, 1 << b)
    total = keep + recv
    out = total[:local_rows]
    for k in range(1, KVH):
        out = out + swap(total[k * local_rows : (k + 1) * local_rows], k * sub)
    return out


def head_partials(query_rows, keys_held, values_held, key_pos, lengths):
    row_count = query_rows.shape[0]
    grouped = query_rows.reshape(row_count, GROUP, HD)
    scores = jnp.einsum(
        "tje,pe->tjp", grouped, keys_held, precision=HIGHEST, preferred_element_type=jnp.float32
    ) * (1.0 / math.sqrt(HD))
    request_ids = jnp.arange(row_count, dtype=jnp.int32) // REQ_TOK
    request_table = jnp.arange(lengths.shape[0], dtype=jnp.int32)
    limits = jnp.sum(
        jnp.where(request_ids[:, None] == request_table[None, :], lengths[None, :], 0), axis=1
    )
    visible = (key_pos[None, :] < limits[:, None])[:, None, :]
    masked = jnp.where(visible, scores, NEG_FILL)
    peak_vals = jnp.max(masked, axis=2)
    weights = jnp.where(visible, jnp.exp(masked - peak_vals[..., None]), 0.0)
    totals = jnp.sum(weights, axis=2)
    mixed_values = jnp.einsum(
        "tjp,pe->tje", weights, values_held, precision=HIGHEST, preferred_element_type=jnp.float32
    )
    return mixed_values.reshape(row_count, GROUP * HD), peak_vals, totals


def by_all_to_all(queries, keys, values, weight, lengths):
    blocks = lax.axis_size("blk")
    position = lax.axis_index("blk")
    local_rows = queries.shape[0]
    total_rows = local_rows * blocks
    key_count = keys.shape[0]
    sub_count = blocks // KVH
    sub_len = key_count // sub_count

    def exchange(x, split, concat):
        return lax.all_to_all(x, "blk", split_axis=split, concat_axis=concat, tiled=True)

    def spread(x):
        split = x.reshape(sub_count, sub_len, KVH, HD).transpose(0, 2, 1, 3)
        return exchange(split.reshape(blocks, sub_len, HD), 0, 0).reshape(blocks * sub_len, HD)

    held_pos = (
        jnp.arange(blocks, dtype=jnp.int32)[:, None] * key_count
        + position // KVH * sub_len
        + jnp.arange(sub_len, dtype=jnp.int32)[None, :]
    ).reshape(blocks * sub_len)
    query_heads = queries.reshape(local_rows, KVH, GROUP * HD).transpose(1, 0, 2)
    query_send = jnp.broadcast_to(query_heads[None], (sub_count, KVH, local_rows, GROUP * HD))
    query_held = exchange(query_send.reshape(blocks, local_rows, GROUP * HD), 0, 0)
    sums, peaks, totals = head_partials(
        query_held.reshape(total_rows, GROUP * HD), spread(keys), spread(values), held_pos, lengths
    )
    sums = exchange(sums, 0, 0).reshape(sub_count, KVH, local_rows, GROUP, HD)
    peaks = exchange(peaks, 0, 0).reshape(sub_count, KVH, local_rows, GROUP)
    totals = exchange(totals, 0, 0).reshape(sub_count, KVH, local_rows, GROUP)
    factor = jnp.exp(peaks - jnp.max(peaks, axis=0)[None])
    numerator = jnp.sum(sums * factor[..., None], axis=0)
    denominator = jnp.sum(totals * factor, axis=0)
    attended = (numerator / denominator[..., None]).transpose(1, 0, 2, 3).reshape(local_rows, H * HD)
    feature_rows = exchange(attended, 1, 0)
    parts = jnp.dot(feature_rows, weight, precision=HIGHEST, preferred_element_type=jnp.float32)
    return jnp.sum(exchange(parts, 0, 0).reshape(blocks, local_rows, weight.shape[1]), axis=0)


def per_device(queries, prefix_keys, prefix_values, out_weight, lengths):
    blocks = lax.axis_size("blk")
    sub = blocks // KVH
    bits = sub.bit_length() - 1
    fits = (
        blocks == KVH << bits
        and bits >= 1
        and GROUP % sub == 0
        and (KVH * queries.shape[0]) % 8 == 0
        and prefix_keys.shape[0] % LANES == 0
    )
    if fits:
        return by_planes(bits, queries, prefix_keys, prefix_values, out_weight, lengths)
    return by_all_to_all(queries, prefix_keys, prefix_values, out_weight, lengths)


def solution(mesh):
    in_specs = (
        P(("groups", "blk"), None),
        P(("groups", "blk"), None),
        P(("groups", "blk"), None),
        P("blk", None),
        P("groups"),
    )
    out_specs = P(("groups", "blk"), None)
    return jax.shard_map(
        per_device, mesh=mesh, in_specs=in_specs, out_specs=out_specs, check_vma=False
    )
```

```python
import functools
import math

import jax
import jax.numpy as jnp
from jax import lax
from jax.experimental import pallas as pl
from jax.experimental.pallas import tpu as pltpu
from jax.sharding import PartitionSpec as P


H = 64
KVH = 4
HD = 128
REQ_TOK = 16
GROUP = H // KVH
LANES = 128

HIGHEST = lax.Precision.HIGHEST
NEG_FILL = -1e30


VMEM = pltpu.VMEM


def reverse_bits(value, bits):
    out = 0
    for b in range(bits):
        out |= ((value >> b) & 1) << (bits - 1 - b)
    return out


def swap_rows(x, size):
    blocks = [x[i * size : (i + 1) * size] for i in range(x.shape[0] // size)]
    return jnp.concatenate([blocks[i ^ 1] for i in range(len(blocks))], axis=0)


def lanes_of(columns, rows):
    lane = lax.broadcasted_iota(jnp.int32, (rows, LANES), 1)
    out = jnp.zeros((rows, LANES), jnp.float32)
    for i, column in enumerate(columns):
        out = jnp.where(lane == i, column, out)
    return out


def pieces_of(x, count):
    out = []
    for _ in range(count):
        out.append(x.astype(jnp.bfloat16))
        x = x - out[-1].astype(jnp.float32)
    return out


def times(a, b, dims=(((1,), (0,)), ((), ()))):
    return lax.dot_general(a, b, dims, preferred_element_type=jnp.float32)


def limit(mib):
    return pltpu.CompilerParams(vmem_limit_bytes=mib << 20)


IN_VMEM = pl.BlockSpec(memory_space=VMEM)
IN_PLACE = pl.BlockSpec(memory_space=pl.ANY)


def in_hbm(x):
    return pltpu.with_memory_space_constraint(x, pltpu.HBM)


def pack_kernel(sub, q_hbm, k_hbm, v_hbm, *refs):
    outs, sems = refs[:-1], refs[-1]
    plane = lax.axis_index("blk") // sub
    keys, wide = k_hbm.shape[0], GROUP * HD
    copies = []
    for step in (2, 3, 1, 0) if KVH == 4 else range(KVH):
        other = plane ^ step
        lanes = pl.ds(pl.multiple_of(other * HD, HD), HD)
        q_lanes = pl.ds(pl.multiple_of(other * wide, wide), wide)
        copies += [
            (k_hbm.at[:, lanes], outs[step].at[pl.ds(0, keys), :]),
            (v_hbm.at[:, lanes], outs[step].at[pl.ds(keys, keys), :]),
            (q_hbm.at[:, q_lanes], outs[KVH + step]),
        ]
    copies = [pltpu.make_async_copy(src, dst, sems.at[i]) for i, (src, dst) in enumerate(copies)]
    for copy in copies:
        copy.start()
    for copy in copies:
        copy.wait()


def pack(sub, queries, keys, values):
    kv = jax.ShapeDtypeStruct((2 * keys.shape[0], HD), jnp.float32)
    q = jax.ShapeDtypeStruct((queries.shape[0], GROUP * HD), jnp.float32)
    out = pl.pallas_call(
        functools.partial(pack_kernel, sub),
        out_shape=[kv] * KVH + [q] * KVH,
        in_specs=[IN_PLACE] * 3,
        out_specs=[IN_VMEM] * (2 * KVH),
        scratch_shapes=[pltpu.SemaphoreType.DMA((3 * KVH,))],
        compiler_params=limit(4),
        name="pack",
    )(in_hbm(queries), in_hbm(keys), in_hbm(values))
    return out[:KVH], out[KVH:]


def split_kernel(tile, w_hbm, high_ref, low_ref, buf, sems):
    chunks = w_hbm.shape[0] // tile
    copies = [
        pltpu.make_async_copy(w_hbm.at[pl.ds(c * tile, tile), :], buf.at[c], sems.at[c])
        for c in range(chunks)
    ]
    for copy in copies:
        copy.start()
    for c in range(chunks):
        copies[c].wait()
        rows = slice(c * tile, (c + 1) * tile)
        high_ref[rows, :], low_ref[rows, :] = pieces_of(buf[c], 2)


def split_weight(weight):
    features, width = weight.shape
    tile = min(features, 64)
    out = jax.ShapeDtypeStruct((features, width), jnp.bfloat16)
    return pl.pallas_call(
        functools.partial(split_kernel, tile),
        out_shape=[out, out],
        in_specs=[IN_PLACE],
        out_specs=[IN_VMEM] * 2,
        scratch_shapes=[
            pltpu.VMEM((features // tile, tile, width), jnp.float32),
            pltpu.SemaphoreType.DMA((features // tile,)),
        ],
        compiler_params=limit(20),
        cost_estimate=pl.CostEstimate(
            flops=8 * features * width, bytes_accessed=8 * features * width, transcendentals=0
        ),
        name="split",
    )(in_hbm(weight))


def attend_kernel(bits, local_rows, key_count, len_ref, *refs):
    sub = 1 << bits
    q_refs, kv_refs = refs[:sub], refs[sub : sub + KVH]
    send_ref, keep_ref = refs[sub + KVH :]
    position = lax.axis_index("blk")
    plane, place = position // sub, position % sub
    part = KVH * local_rows
    rows = part * sub
    per_owner = GROUP // sub
    held = key_count * KVH

    row = lax.broadcasted_iota(jnp.int32, (rows, 1), 0)
    order = row // part
    within = row % part
    rel = (within // local_rows) * sub
    for b in range(bits):
        rel = rel + ((order >> (bits - 1 - b)) & 1) * (1 << b)
    token = (position ^ rel) * local_rows + within % local_rows
    request = token // REQ_TOK
    limits = jnp.zeros((rows, 1), jnp.int32)
    for i in range(len_ref.shape[0]):
        limits = jnp.where(request == i, len_ref[i], limits)
    at = lax.broadcasted_iota(jnp.int32, (1, held), 1)
    source = (plane ^ (at // key_count)) * sub + place
    visible = (source * key_count + at % key_count) < limits

    keys = jnp.concatenate([r[:key_count, :] for r in kv_refs], axis=0)
    values = jnp.concatenate([r[key_count:, :] for r in kv_refs], axis=0)
    k1, k2, k3 = pieces_of(keys, 3)
    k12, k31 = jnp.concatenate([k1, k2], axis=1), jnp.concatenate([k3, k1], axis=1)
    v1, v2 = pieces_of(values, 2)
    v12 = jnp.concatenate([v1, v2], axis=1)
    both = (((1,), (1,)), ((), ()))
    scale = 1.0 / math.sqrt(HD)

    half = GROUP // 2
    cross = jnp.broadcast_to(visible[None], (half, rows, held))
    for ref, start in ((send_ref, half), (keep_ref, 0)):
        heads = []
        for head in range(start, start + half):
            owner = place ^ reverse_bits(head // per_owner, bits)
            lanes = pl.ds(pl.multiple_of((owner * per_owner + head % per_owner) * HD, HD), HD)
            heads += [q_ref[:, lanes] for q_ref in q_refs]
        q1, q2, q3 = pieces_of(jnp.concatenate(heads, axis=0), 3)
        q11, q22 = jnp.concatenate([q1, q1], axis=1), jnp.concatenate([q2, q2], axis=1)
        q13 = jnp.concatenate([q1, q3], axis=1)
        scores = times(q11, k12, both) + (times(q22, k12, both) + times(q13, k31, both))
        scores = scores.reshape(half, rows, held) * scale
        masked = jnp.where(cross, scores, NEG_FILL)
        peak = jnp.max(masked, axis=2, keepdims=True)
        weights = jnp.where(cross, jnp.exp(masked - peak), 0.0)
        total = jnp.sum(weights, axis=2, keepdims=True)
        w1, w2 = pieces_of(weights.reshape(half * rows, held), 2)
        wide = times(w1, v12)
        sums = wide[:, :HD] + (wide[:, HD:] + times(w2, v1))
        for i in range(half):
            ref[:, i * HD : (i + 1) * HD] = sums[i * rows : (i + 1) * rows]
        stats = [peak[i] for i in range(half)] + [total[i] for i in range(half)]
        ref[:, half * HD :] = lanes_of(stats, rows)


def attend(bits, local_rows, lengths, q_parts, kv_held):
    sub = 1 << bits
    rows = KVH * local_rows * sub
    out = jax.ShapeDtypeStruct((rows, GROUP // 2 * HD + LANES), jnp.float32)
    return pl.pallas_call(
        functools.partial(attend_kernel, bits, local_rows, kv_held[0].shape[0] // 2),
        out_shape=[out, out],
        in_specs=[pl.BlockSpec(memory_space=pltpu.SMEM)] + [IN_VMEM] * (sub + KVH),
        out_specs=[IN_VMEM] * 2,
        compiler_params=limit(16),
        name="attend",
    )(lengths, *q_parts, *kv_held)


def merged(keep_ref, recv_ref, swap):
    heads = (keep_ref.shape[1] - LANES) // HD
    mine, other = keep_ref[:, heads * HD :], swap_rows(recv_ref[:, heads * HD :], swap)
    sums, peaks, totals = [], [], []
    for i in range(heads):
        peak_a, peak_b = mine[:, i : i + 1], other[:, i : i + 1]
        peak = jnp.maximum(peak_a, peak_b)
        factor_a, factor_b = jnp.exp(peak_a - peak), jnp.exp(peak_b - peak)
        cols = slice(i * HD, (i + 1) * HD)
        sums.append(keep_ref[:, cols] * factor_a + swap_rows(recv_ref[:, cols], swap) * factor_b)
        peaks.append(peak)
        totals.append(
            mine[:, heads + i : heads + i + 1] * factor_a + other[:, heads + i : heads + i + 1] * factor_b
        )
    return sums, peaks, totals


def merge_kernel(swap, keep_ref, recv_ref, send_out, keep_out):
    sums, peaks, totals = merged(keep_ref, recv_ref, swap)
    half = len(sums) // 2
    for start, ref in ((0, keep_out), (half, send_out)):
        for i in range(half):
            ref[:, i * HD : (i + 1) * HD] = sums[start + i]
        stats = peaks[start : start + half] + totals[start : start + half]
        ref[:, half * HD :] = lanes_of(stats, keep_ref.shape[0])


def merge(swap, keep, recv):
    rows, width = keep.shape
    half = (width - LANES) // HD // 2
    out = jax.ShapeDtypeStruct((rows, half * HD + LANES), jnp.float32)
    return pl.pallas_call(
        functools.partial(merge_kernel, swap),
        out_shape=[out, out],
        in_specs=[IN_VMEM] * 2,
        out_specs=[IN_VMEM] * 2,
        compiler_params=limit(4),
        name="merge",
    )(keep, recv)


def project_kernel(swap, tile, keep_ref, recv_ref, high_ref, low_ref, send_out, keep_out):
    sums, _, totals = merged(keep_ref, recv_ref, swap)
    attended = jnp.concatenate([a / t for a, t in zip(sums, totals)], axis=1)
    rows = attended.shape[0]
    half = rows // 2
    a1, a2 = pieces_of(attended, 2)
    a12 = jnp.concatenate([a1, a2], axis=0)
    for c in range(high_ref.shape[1] // tile):
        cols = slice(c * tile, (c + 1) * tile)
        top = times(a12, high_ref[:, cols])
        out = top[:rows] + (top[rows:] + times(a1, low_ref[:, cols]))
        keep_out[:, cols] = out[:half]
        send_out[:, cols] = out[half:]


def project(swap, keep, recv, high, low):
    width = high.shape[1]
    out = jax.ShapeDtypeStruct((keep.shape[0] // 2, width), jnp.float32)
    return pl.pallas_call(
        functools.partial(project_kernel, swap, min(width, 512)),
        out_shape=[out, out],
        in_specs=[IN_VMEM] * 4,
        out_specs=[IN_VMEM] * 2,
        compiler_params=limit(16),
        name="project",
    )(keep, recv, high, low)


def by_planes(bits, queries, keys, values, weight, lengths):
    blocks = lax.axis_size("blk")
    sub = 1 << bits
    local_rows = queries.shape[0]
    part = KVH * local_rows

    def swap(x, mask):
        return lax.ppermute(x, "blk", [(i, i ^ mask) for i in range(blocks)])

    kv_send, q_send = pack(sub, queries, keys, values)
    kv_held = [kv_send[0]] + [swap(kv_send[k], k * sub) for k in range(1, KVH)]
    q_rows = [q_send[0]] + [swap(q_send[k], k * sub) for k in range(1, KVH)]
    q_parts = [jnp.concatenate(q_rows, axis=0)]
    for b in reversed(range(bits)):
        q_parts = q_parts + [swap(x, 1 << b) for x in q_parts]
    high, low = split_weight(weight)

    send, keep = attend(bits, local_rows, lengths, q_parts, kv_held)
    for b in range(bits - 1):
        send, keep = merge(part << (bits - 1 - b), keep, swap(send, 1 << b))
    send, keep = project(part, keep, swap(send, 1 << (bits - 1)), high, low)

    recv = swap(send, 1)
    for b in range(1, bits):
        half = keep.shape[0] // 2
        send = keep[half:] + recv[half:]
        keep = keep[:half] + recv[:half]
        recv = swap(send, 1 << b)
    total = keep + recv
    out = total[:local_rows]
    for k in range(1, KVH):
        out = out + swap(total[k * local_rows : (k + 1) * local_rows], k * sub)
    return out


def head_partials(query_rows, keys_held, values_held, key_pos, lengths):
    row_count = query_rows.shape[0]
    grouped = query_rows.reshape(row_count, GROUP, HD)
    scores = jnp.einsum(
        "tje,pe->tjp", grouped, keys_held, precision=HIGHEST, preferred_element_type=jnp.float32
    ) * (1.0 / math.sqrt(HD))
    request_ids = jnp.arange(row_count, dtype=jnp.int32) // REQ_TOK
    request_table = jnp.arange(lengths.shape[0], dtype=jnp.int32)
    limits = jnp.sum(
        jnp.where(request_ids[:, None] == request_table[None, :], lengths[None, :], 0), axis=1
    )
    visible = (key_pos[None, :] < limits[:, None])[:, None, :]
    masked = jnp.where(visible, scores, NEG_FILL)
    peak_vals = jnp.max(masked, axis=2)
    weights = jnp.where(visible, jnp.exp(masked - peak_vals[..., None]), 0.0)
    totals = jnp.sum(weights, axis=2)
    mixed_values = jnp.einsum(
        "tjp,pe->tje", weights, values_held, precision=HIGHEST, preferred_element_type=jnp.float32
    )
    return mixed_values.reshape(row_count, GROUP * HD), peak_vals, totals


def by_all_to_all(queries, keys, values, weight, lengths):
    blocks = lax.axis_size("blk")
    position = lax.axis_index("blk")
    local_rows = queries.shape[0]
    total_rows = local_rows * blocks
    key_count = keys.shape[0]
    sub_count = blocks // KVH
    sub_len = key_count // sub_count

    def exchange(x, split, concat):
        return lax.all_to_all(x, "blk", split_axis=split, concat_axis=concat, tiled=True)

    def spread(x):
        split = x.reshape(sub_count, sub_len, KVH, HD).transpose(0, 2, 1, 3)
        return exchange(split.reshape(blocks, sub_len, HD), 0, 0).reshape(blocks * sub_len, HD)

    held_pos = (
        jnp.arange(blocks, dtype=jnp.int32)[:, None] * key_count
        + position // KVH * sub_len
        + jnp.arange(sub_len, dtype=jnp.int32)[None, :]
    ).reshape(blocks * sub_len)
    query_heads = queries.reshape(local_rows, KVH, GROUP * HD).transpose(1, 0, 2)
    query_send = jnp.broadcast_to(query_heads[None], (sub_count, KVH, local_rows, GROUP * HD))
    query_held = exchange(query_send.reshape(blocks, local_rows, GROUP * HD), 0, 0)
    sums, peaks, totals = head_partials(
        query_held.reshape(total_rows, GROUP * HD), spread(keys), spread(values), held_pos, lengths
    )
    sums = exchange(sums, 0, 0).reshape(sub_count, KVH, local_rows, GROUP, HD)
    peaks = exchange(peaks, 0, 0).reshape(sub_count, KVH, local_rows, GROUP)
    totals = exchange(totals, 0, 0).reshape(sub_count, KVH, local_rows, GROUP)
    factor = jnp.exp(peaks - jnp.max(peaks, axis=0)[None])
    numerator = jnp.sum(sums * factor[..., None], axis=0)
    denominator = jnp.sum(totals * factor, axis=0)
    attended = (numerator / denominator[..., None]).transpose(1, 0, 2, 3).reshape(local_rows, H * HD)
    feature_rows = exchange(attended, 1, 0)
    parts = jnp.dot(feature_rows, weight, precision=HIGHEST, preferred_element_type=jnp.float32)
    return jnp.sum(exchange(parts, 0, 0).reshape(blocks, local_rows, weight.shape[1]), axis=0)


def per_device(queries, prefix_keys, prefix_values, out_weight, lengths):
    blocks = lax.axis_size("blk")
    sub = blocks // KVH
    bits = sub.bit_length() - 1
    fits = (
        blocks == KVH << bits
        and bits >= 1
        and GROUP % sub == 0
        and (KVH * queries.shape[0]) % 8 == 0
        and prefix_keys.shape[0] % LANES == 0
    )
    if fits:
        return by_planes(bits, queries, prefix_keys, prefix_values, out_weight, lengths)
    return by_all_to_all(queries, prefix_keys, prefix_values, out_weight, lengths)


def solution(mesh):
    in_specs = (
        P(("groups", "blk"), None),
        P(("groups", "blk"), None),
        P(("groups", "blk"), None),
        P("blk", None),
        P("groups"),
    )
    out_specs = P(("groups", "blk"), None)
    return jax.shard_map(
        per_device, mesh=mesh, in_specs=in_specs, out_specs=out_specs, check_vma=False
    )
```

```python
import functools
import math

import jax
import jax.numpy as jnp
from jax import lax
from jax.experimental import pallas as pl
from jax.experimental.pallas import tpu as pltpu
from jax.sharding import PartitionSpec as P


H = 64
KVH = 4
HD = 128
REQ_TOK = 16
GROUP = H // KVH
PLANE_BITS = KVH.bit_length() - 1
LANES = 128

HIGHEST = lax.Precision.HIGHEST
NEG_FILL = -1e30


VMEM = pltpu.VMEM


def reverse_bits(value, bits):
    out = 0
    for b in range(bits):
        out |= ((value >> b) & 1) << (bits - 1 - b)
    return out


def relative(order, bits):
    out = 0
    for b in range(PLANE_BITS):
        out = out + (((order >> (PLANE_BITS - 1 - b)) & 1) << (bits + b))
    for b in range(bits):
        out = out + (((order >> (PLANE_BITS + bits - 1 - b)) & 1) << b)
    return out


def swap_rows(x, size):
    blocks = [x[i * size : (i + 1) * size] for i in range(x.shape[0] // size)]
    return jnp.concatenate([blocks[i ^ 1] for i in range(len(blocks))], axis=0)


def lanes_of(columns, rows):
    lane = lax.broadcasted_iota(jnp.int32, (rows, LANES), 1)
    out = jnp.zeros((rows, LANES), jnp.float32)
    for i, column in enumerate(columns):
        out = jnp.where(lane == i, column, out)
    return out


def pieces_of(x, count):
    out = []
    for _ in range(count):
        out.append(x.astype(jnp.bfloat16))
        x = x - out[-1].astype(jnp.float32)
    return out


def times(a, b, dims=(((1,), (0,)), ((), ()))):
    return lax.dot_general(a, b, dims, preferred_element_type=jnp.float32)


def limit(mib):
    return pltpu.CompilerParams(vmem_limit_bytes=mib << 20)


IN_VMEM = pl.BlockSpec(memory_space=VMEM)
IN_PLACE = pl.BlockSpec(memory_space=pl.ANY)


def in_hbm(x):
    return pltpu.with_memory_space_constraint(x, pltpu.HBM)


def pack_kernel(bits, len_hbm, q_hbm, k_hbm, v_hbm, *refs):
    kv_outs, q_outs, (limit_out, len_ref, sems) = refs[:KVH], refs[KVH:-3], refs[-3:]
    position = lax.axis_index("blk")
    plane = position >> bits
    keys, wide, half = k_hbm.shape[0], GROUP * HD, KVH // 2
    copies = [(len_hbm, len_ref)]
    for step in reversed(range(KVH)):
        other = plane ^ step
        q_out = q_outs[0].at[:, pl.ds((step - half) * wide, wide)] if step >= half else q_outs[1 + step]
        copies.append((q_hbm.at[:, pl.ds(pl.multiple_of(other * wide, wide), wide)], q_out))
    for step in reversed(range(KVH)):
        lanes = pl.ds(pl.multiple_of((plane ^ step) * HD, HD), HD)
        copies.append((k_hbm.at[:, lanes], kv_outs[step].at[pl.ds(0, keys), :]))
        copies.append((v_hbm.at[:, lanes], kv_outs[step].at[pl.ds(keys, keys), :]))
    copies = [pltpu.make_async_copy(src, dst, sems.at[i]) for i, (src, dst) in enumerate(copies)]
    for copy in copies:
        copy.start()
    local_rows = q_hbm.shape[0]
    row = lax.broadcasted_iota(jnp.int32, limit_out.shape, 0)
    token = (position ^ relative(row // local_rows, bits)) * local_rows + row % local_rows
    request = token // REQ_TOK
    copies[0].wait()
    limits = jnp.zeros(limit_out.shape, jnp.int32)
    for i in range(len_ref.shape[0]):
        limits = jnp.where(request == i, len_ref[i], limits)
    limit_out[...] = limits
    for copy in copies[1:]:
        copy.wait()


def pack(bits, lengths, queries, keys, values):
    local_rows = queries.shape[0]
    kv = jax.ShapeDtypeStruct((2 * keys.shape[0], HD), jnp.float32)
    q = jax.ShapeDtypeStruct((local_rows, GROUP * HD), jnp.float32)
    q_high = jax.ShapeDtypeStruct((local_rows, KVH // 2 * GROUP * HD), jnp.float32)
    limits = jax.ShapeDtypeStruct(((KVH << bits) * local_rows, LANES), jnp.int32)
    out = pl.pallas_call(
        functools.partial(pack_kernel, bits),
        out_shape=[kv] * KVH + [q_high] + [q] * (KVH // 2) + [limits],
        in_specs=[IN_PLACE] * 4,
        out_specs=[IN_VMEM] * (KVH + KVH // 2 + 2),
        scratch_shapes=[
            pltpu.SMEM(lengths.shape, jnp.int32),
            pltpu.SemaphoreType.DMA((1 + 3 * KVH,)),
        ],
        compiler_params=limit(4),
        name="pack",
    )(*map(in_hbm, (lengths, queries, keys, values)))
    return out[:KVH], out[KVH:-1], out[-1]


def split_kernel(first, tile, w_hbm, high_ref, low_ref, buf, sems):
    chunks = buf.shape[0]
    copies = [
        pltpu.make_async_copy(w_hbm.at[pl.ds(first + c * tile, tile), :], buf.at[c], sems.at[c])
        for c in range(chunks)
    ]
    for copy in copies:
        copy.start()
    for c in range(chunks):
        copies[c].wait()
        rows = slice(c * tile, (c + 1) * tile)
        high_ref[rows, :], low_ref[rows, :] = pieces_of(buf[c], 2)


def split_weight(weight, first, count):
    width = weight.shape[1]
    tile = min(count, 64)
    out = jax.ShapeDtypeStruct((count, width), jnp.bfloat16)
    return pl.pallas_call(
        functools.partial(split_kernel, first, tile),
        out_shape=[out, out],
        in_specs=[IN_PLACE],
        out_specs=[IN_VMEM] * 2,
        scratch_shapes=[
            pltpu.VMEM((count // tile, tile, width), jnp.float32),
            pltpu.SemaphoreType.DMA((count // tile,)),
        ],
        compiler_params=limit(12),
        cost_estimate=pl.CostEstimate(
            flops=8 * count * width, bytes_accessed=8 * count * width, transcendentals=0
        ),
        name="split",
    )(in_hbm(weight))


def attend_kernel(bits, key_count, limit_ref, *refs):
    sub = 1 << bits
    q_refs, kv_refs = refs[:sub], refs[sub : sub + KVH]
    send_ref, keep_ref = refs[sub + KVH :]
    position = lax.axis_index("blk")
    plane, place = position // sub, position % sub
    rows = limit_ref.shape[0]
    per_owner = GROUP // sub
    held = key_count * KVH

    at = lax.broadcasted_iota(jnp.int32, (1, held), 1)
    source = (plane ^ (at // key_count)) * sub + place
    visible = (source * key_count + at % key_count) < limit_ref[:, :1]

    keys = jnp.concatenate([r[:key_count, :] for r in kv_refs], axis=0)
    values = jnp.concatenate([r[key_count:, :] for r in kv_refs], axis=0)
    k1, k2, k3 = pieces_of(keys, 3)
    k12, k31 = jnp.concatenate([k1, k2], axis=1), jnp.concatenate([k3, k1], axis=1)
    v1, v2 = pieces_of(values, 2)
    v12 = jnp.concatenate([v1, v2], axis=1)
    both = (((1,), (1,)), ((), ()))
    scale = 1.0 / math.sqrt(HD)

    half = GROUP // 2
    cross = jnp.broadcast_to(visible[None], (half, rows, held))
    for ref, start in ((send_ref, half), (keep_ref, 0)):
        heads = []
        for head in range(start, start + half):
            owner = place ^ reverse_bits(head // per_owner, bits)
            lanes = pl.ds(pl.multiple_of((owner * per_owner + head % per_owner) * HD, HD), HD)
            heads += [q_ref[:, lanes] for q_ref in q_refs]
        q1, q2, q3 = pieces_of(jnp.concatenate(heads, axis=0), 3)
        q11, q22 = jnp.concatenate([q1, q1], axis=1), jnp.concatenate([q2, q2], axis=1)
        q13 = jnp.concatenate([q1, q3], axis=1)
        scores = times(q11, k12, both) + (times(q22, k12, both) + times(q13, k31, both))
        scores = scores.reshape(half, rows, held) * scale
        masked = jnp.where(cross, scores, NEG_FILL)
        peak = jnp.max(masked, axis=2, keepdims=True)
        weights = jnp.where(cross, jnp.exp(masked - peak), 0.0)
        total = jnp.sum(weights, axis=2, keepdims=True)
        w1, w2 = pieces_of(weights.reshape(half * rows, held), 2)
        wide = times(w1, v12)
        sums = wide[:, :HD] + (wide[:, HD:] + times(w2, v1))
        for i in range(half):
            ref[:, i * HD : (i + 1) * HD] = sums[i * rows : (i + 1) * rows]
        stats = [peak[i] for i in range(half)] + [total[i] for i in range(half)]
        ref[:, half * HD :] = lanes_of(stats, rows)


def attend(bits, limits, q_parts, kv_held):
    out = jax.ShapeDtypeStruct((limits.shape[0], GROUP // 2 * HD + LANES), jnp.float32)
    return pl.pallas_call(
        functools.partial(attend_kernel, bits, kv_held[0].shape[0] // 2),
        out_shape=[out, out],
        in_specs=[IN_VMEM] * (1 + len(q_parts) + KVH),
        out_specs=[IN_VMEM] * 2,
        compiler_params=limit(16),
        name="attend",
    )(limits, *q_parts, *kv_held)


def merged(keep_ref, recv_ref, swap):
    heads = (keep_ref.shape[1] - LANES) // HD
    mine, other = keep_ref[:, heads * HD :], swap_rows(recv_ref[:, heads * HD :], swap)
    sums, peaks, totals = [], [], []
    for i in range(heads):
        peak_a, peak_b = mine[:, i : i + 1], other[:, i : i + 1]
        peak = jnp.maximum(peak_a, peak_b)
        factor_a, factor_b = jnp.exp(peak_a - peak), jnp.exp(peak_b - peak)
        cols = slice(i * HD, (i + 1) * HD)
        sums.append(keep_ref[:, cols] * factor_a + swap_rows(recv_ref[:, cols], swap) * factor_b)
        peaks.append(peak)
        totals.append(
            mine[:, heads + i : heads + i + 1] * factor_a + other[:, heads + i : heads + i + 1] * factor_b
        )
    return sums, peaks, totals


def merge_kernel(swap, keep_ref, recv_ref, send_out, keep_out):
    sums, peaks, totals = merged(keep_ref, recv_ref, swap)
    half = len(sums) // 2
    for start, ref in ((0, keep_out), (half, send_out)):
        for i in range(half):
            ref[:, i * HD : (i + 1) * HD] = sums[start + i]
        stats = peaks[start : start + half] + totals[start : start + half]
        ref[:, half * HD :] = lanes_of(stats, keep_ref.shape[0])


def merge(swap, keep, recv):
    rows, width = keep.shape
    half = (width - LANES) // HD // 2
    out = jax.ShapeDtypeStruct((rows, half * HD + LANES), jnp.float32)
    return pl.pallas_call(
        functools.partial(merge_kernel, swap),
        out_shape=[out, out],
        in_specs=[IN_VMEM] * 2,
        out_specs=[IN_VMEM] * 2,
        compiler_params=limit(4),
        name="merge",
    )(keep, recv)


def project_kernel(swap, tile, keep_ref, recv_ref, *refs):
    piece_refs, (send_out, keep_out) = refs[:-2], refs[-2:]
    sums, _, totals = merged(keep_ref, recv_ref, swap)
    attended = jnp.concatenate([a / t for a, t in zip(sums, totals)], axis=1)
    rows = attended.shape[0]
    half = rows // 2
    a1, a2 = pieces_of(attended, 2)
    a12 = jnp.concatenate([a1, a2], axis=0)
    for c in range(keep_out.shape[1] // tile):
        cols = slice(c * tile, (c + 1) * tile)
        out, first = 0.0, 0
        for high_ref, low_ref in zip(piece_refs[::2], piece_refs[1::2]):
            used = slice(first, first + high_ref.shape[0])
            first = used.stop
            top = times(a12[:, used], high_ref[:, cols])
            out = out + (top[:rows] + (top[rows:] + times(a1[:, used], low_ref[:, cols])))
        keep_out[:, cols] = out[:half]
        send_out[:, cols] = out[half:]


def project(swap, keep, recv, pieces):
    width = pieces[0].shape[1]
    out = jax.ShapeDtypeStruct((keep.shape[0] // 2, width), jnp.float32)
    return pl.pallas_call(
        functools.partial(project_kernel, swap, min(width, 512)),
        out_shape=[out, out],
        in_specs=[IN_VMEM] * (2 + len(pieces)),
        out_specs=[IN_VMEM] * 2,
        compiler_params=limit(16),
        name="project",
    )(keep, recv, *pieces)


def by_planes(bits, queries, keys, values, weight, lengths):
    blocks = lax.axis_size("blk")
    sub = 1 << bits
    local_rows = queries.shape[0]
    part = KVH * local_rows

    def swap(x, mask):
        return lax.ppermute(x, "blk", [(i, i ^ mask) for i in range(blocks)])

    kv_send, q_send, limits = pack(bits, lengths, queries, keys, values)
    kv_held = [kv_send[0]] + [swap(kv_send[k], k * sub) for k in range(1, KVH)]
    wide = GROUP * HD
    q_rows = [[q] for q in q_send[1:]]
    q_out = q_send[0]
    for b in reversed(range(PLANE_BITS)):
        q_in = swap(q_out, sub << b)
        count = len(q_rows[0])
        got = [q_in[:, i * wide : (i + 1) * wide] for i in range(q_in.shape[1] // wide)]
        q_rows = [rows + got[t * count : (t + 1) * count] for t, rows in enumerate(q_rows)]
        high = q_rows[len(q_rows) // 2 :]
        if b:
            q_out = jnp.concatenate([piece for rows in high for piece in rows], axis=1)
            q_rows = q_rows[: len(q_rows) // 2]
    q_parts = [jnp.concatenate(q_rows[0], axis=0)]
    for b in reversed(range(bits)):
        q_parts = q_parts + [swap(x, 1 << b) for x in q_parts]
    features = weight.shape[0]
    pieces = []
    for i in range(2):
        pieces += split_weight(weight, i * features // 2, features // 2)

    send, keep = attend(bits, limits, q_parts, kv_held)
    for b in range(bits - 1):
        send, keep = merge(part << (bits - 1 - b), keep, swap(send, 1 << b))
    send, keep = project(part, keep, swap(send, 1 << (bits - 1)), pieces)

    recv = swap(send, 1)
    for b in range(1, bits):
        half = keep.shape[0] // 2
        send = keep[half:] + recv[half:]
        keep = keep[:half] + recv[:half]
        recv = swap(send, 1 << b)
    total = keep + recv
    out = total[:local_rows]
    for order in range(1, KVH):
        k = relative(order, 0)
        out = out + swap(total[order * local_rows : (order + 1) * local_rows], k * sub)
    return out


def head_partials(query_rows, keys_held, values_held, key_pos, lengths):
    row_count = query_rows.shape[0]
    grouped = query_rows.reshape(row_count, GROUP, HD)
    scores = jnp.einsum(
        "tje,pe->tjp", grouped, keys_held, precision=HIGHEST, preferred_element_type=jnp.float32
    ) * (1.0 / math.sqrt(HD))
    request_ids = jnp.arange(row_count, dtype=jnp.int32) // REQ_TOK
    request_table = jnp.arange(lengths.shape[0], dtype=jnp.int32)
    limits = jnp.sum(
        jnp.where(request_ids[:, None] == request_table[None, :], lengths[None, :], 0), axis=1
    )
    visible = (key_pos[None, :] < limits[:, None])[:, None, :]
    masked = jnp.where(visible, scores, NEG_FILL)
    peak_vals = jnp.max(masked, axis=2)
    weights = jnp.where(visible, jnp.exp(masked - peak_vals[..., None]), 0.0)
    totals = jnp.sum(weights, axis=2)
    mixed_values = jnp.einsum(
        "tjp,pe->tje", weights, values_held, precision=HIGHEST, preferred_element_type=jnp.float32
    )
    return mixed_values.reshape(row_count, GROUP * HD), peak_vals, totals


def by_all_to_all(queries, keys, values, weight, lengths):
    blocks = lax.axis_size("blk")
    position = lax.axis_index("blk")
    local_rows = queries.shape[0]
    total_rows = local_rows * blocks
    key_count = keys.shape[0]
    sub_count = blocks // KVH
    sub_len = key_count // sub_count

    def exchange(x, split, concat):
        return lax.all_to_all(x, "blk", split_axis=split, concat_axis=concat, tiled=True)

    def spread(x):
        split = x.reshape(sub_count, sub_len, KVH, HD).transpose(0, 2, 1, 3)
        return exchange(split.reshape(blocks, sub_len, HD), 0, 0).reshape(blocks * sub_len, HD)

    held_pos = (
        jnp.arange(blocks, dtype=jnp.int32)[:, None] * key_count
        + position // KVH * sub_len
        + jnp.arange(sub_len, dtype=jnp.int32)[None, :]
    ).reshape(blocks * sub_len)
    query_heads = queries.reshape(local_rows, KVH, GROUP * HD).transpose(1, 0, 2)
    query_send = jnp.broadcast_to(query_heads[None], (sub_count, KVH, local_rows, GROUP * HD))
    query_held = exchange(query_send.reshape(blocks, local_rows, GROUP * HD), 0, 0)
    sums, peaks, totals = head_partials(
        query_held.reshape(total_rows, GROUP * HD), spread(keys), spread(values), held_pos, lengths
    )
    sums = exchange(sums, 0, 0).reshape(sub_count, KVH, local_rows, GROUP, HD)
    peaks = exchange(peaks, 0, 0).reshape(sub_count, KVH, local_rows, GROUP)
    totals = exchange(totals, 0, 0).reshape(sub_count, KVH, local_rows, GROUP)
    factor = jnp.exp(peaks - jnp.max(peaks, axis=0)[None])
    numerator = jnp.sum(sums * factor[..., None], axis=0)
    denominator = jnp.sum(totals * factor, axis=0)
    attended = (numerator / denominator[..., None]).transpose(1, 0, 2, 3).reshape(local_rows, H * HD)
    feature_rows = exchange(attended, 1, 0)
    parts = jnp.dot(feature_rows, weight, precision=HIGHEST, preferred_element_type=jnp.float32)
    return jnp.sum(exchange(parts, 0, 0).reshape(blocks, local_rows, weight.shape[1]), axis=0)


def per_device(queries, prefix_keys, prefix_values, out_weight, lengths):
    blocks = lax.axis_size("blk")
    sub = blocks // KVH
    bits = sub.bit_length() - 1
    fits = (
        blocks == KVH << bits
        and bits >= 1
        and GROUP % sub == 0
        and (KVH * queries.shape[0]) % 8 == 0
        and prefix_keys.shape[0] % LANES == 0
    )
    if fits:
        return by_planes(bits, queries, prefix_keys, prefix_values, out_weight, lengths)
    return by_all_to_all(queries, prefix_keys, prefix_values, out_weight, lengths)


def solution(mesh):
    in_specs = (
        P(("groups", "blk"), None),
        P(("groups", "blk"), None),
        P(("groups", "blk"), None),
        P("blk", None),
        P("groups"),
    )
    out_specs = P(("groups", "blk"), None)
    return jax.shard_map(
        per_device, mesh=mesh, in_specs=in_specs, out_specs=out_specs, check_vma=False
    )
```

```python
import functools
import math

import jax
import jax.numpy as jnp
from jax import lax
from jax.experimental import pallas as pl
from jax.experimental.pallas import tpu as pltpu
from jax.sharding import PartitionSpec as P


H = 64
KVH = 4
HD = 128
REQ_TOK = 16
GROUP = H // KVH
PLANE_BITS = KVH.bit_length() - 1
LANES = 128

HIGHEST = lax.Precision.HIGHEST
NEG_FILL = -1e30


VMEM = pltpu.VMEM


def reverse_bits(value, bits):
    out = 0
    for b in range(bits):
        out |= ((value >> b) & 1) << (bits - 1 - b)
    return out


def relative(order, bits):
    out = 0
    for b in range(PLANE_BITS):
        out = out + (((order >> (PLANE_BITS - 1 - b)) & 1) << (bits + b))
    for b in range(bits):
        out = out + (((order >> (PLANE_BITS + bits - 1 - b)) & 1) << b)
    return out


def swap_rows(x, size):
    blocks = [x[i * size : (i + 1) * size] for i in range(x.shape[0] // size)]
    return jnp.concatenate([blocks[i ^ 1] for i in range(len(blocks))], axis=0)


def lanes_of(columns, rows):
    lane = lax.broadcasted_iota(jnp.int32, (rows, LANES), 1)
    out = jnp.zeros((rows, LANES), jnp.float32)
    for i, column in enumerate(columns):
        out = jnp.where(lane == i, column, out)
    return out


def pieces_of(x, count):
    out = []
    for _ in range(count):
        out.append(x.astype(jnp.bfloat16))
        x = x - out[-1].astype(jnp.float32)
    return out


def times(a, b, dims=(((1,), (0,)), ((), ()))):
    return lax.dot_general(a, b, dims, preferred_element_type=jnp.float32)


def limit(mib):
    return pltpu.CompilerParams(vmem_limit_bytes=mib << 20)


IN_VMEM = pl.BlockSpec(memory_space=VMEM)
IN_PLACE = pl.BlockSpec(memory_space=pl.ANY)


def in_hbm(x):
    return pltpu.with_memory_space_constraint(x, pltpu.HBM)


def run_copies(pairs, sems):
    copies = [pltpu.make_async_copy(src, dst, sems.at[i]) for i, (src, dst) in enumerate(pairs)]
    for copy in copies:
        copy.start()
    return copies


def pack_q_kernel(bits, len_hbm, q_hbm, *refs):
    q_outs, (limit_out, len_ref, sems) = refs[:-3], refs[-3:]
    position = lax.axis_index("blk")
    wide, half = GROUP * HD, KVH // 2
    pairs = [(len_hbm, len_ref)]
    for step in reversed(range(KVH)):
        lanes = pl.ds(pl.multiple_of(((position >> bits) ^ step) * wide, wide), wide)
        q_out = q_outs[0].at[:, pl.ds((step - half) * wide, wide)] if step >= half else q_outs[1 + step]
        pairs.append((q_hbm.at[:, lanes], q_out))
    copies = run_copies(pairs, sems)
    local_rows = q_hbm.shape[0]
    row = lax.broadcasted_iota(jnp.int32, limit_out.shape, 0)
    token = (position ^ relative(row // local_rows, bits)) * local_rows + row % local_rows
    request = token // REQ_TOK
    copies[0].wait()
    limits = jnp.zeros(limit_out.shape, jnp.int32)
    for i in range(len_ref.shape[0]):
        limits = jnp.where(request == i, len_ref[i], limits)
    limit_out[...] = limits
    for copy in copies[1:]:
        copy.wait()


def pack_q(bits, lengths, queries):
    local_rows, wide = queries.shape[0], GROUP * HD
    q_high = jax.ShapeDtypeStruct((local_rows, KVH // 2 * wide), jnp.float32)
    q = jax.ShapeDtypeStruct((local_rows, wide), jnp.float32)
    limits = jax.ShapeDtypeStruct(((KVH << bits) * local_rows, LANES), jnp.int32)
    out = pl.pallas_call(
        functools.partial(pack_q_kernel, bits),
        out_shape=[q_high] + [q] * (KVH // 2) + [limits],
        in_specs=[IN_PLACE] * 2,
        out_specs=[IN_VMEM] * (KVH // 2 + 2),
        scratch_shapes=[pltpu.SMEM(lengths.shape, jnp.int32), pltpu.SemaphoreType.DMA((1 + KVH,))],
        compiler_params=limit(4),
        name="pack_q",
    )(in_hbm(lengths), in_hbm(queries))
    return out[:-1], out[-1]


def pack_kv_kernel(bits, k_hbm, v_hbm, *refs):
    kv_outs, sems = refs[:-1], refs[-1]
    plane = lax.axis_index("blk") >> bits
    keys = k_hbm.shape[0]
    pairs = []
    for step in reversed(range(KVH)):
        lanes = pl.ds(pl.multiple_of((plane ^ step) * HD, HD), HD)
        pairs.append((k_hbm.at[:, lanes], kv_outs[step].at[pl.ds(0, keys), :]))
        pairs.append((v_hbm.at[:, lanes], kv_outs[step].at[pl.ds(keys, keys), :]))
    for copy in run_copies(pairs, sems):
        copy.wait()


def pack_kv(bits, keys, values):
    kv = jax.ShapeDtypeStruct((2 * keys.shape[0], HD), jnp.float32)
    return pl.pallas_call(
        functools.partial(pack_kv_kernel, bits),
        out_shape=[kv] * KVH,
        in_specs=[IN_PLACE] * 2,
        out_specs=[IN_VMEM] * KVH,
        scratch_shapes=[pltpu.SemaphoreType.DMA((2 * KVH,))],
        compiler_params=limit(4),
        cost_estimate=pl.CostEstimate(flops=0, bytes_accessed=16 * keys.size, transcendentals=0),
        name="pack_kv",
    )(in_hbm(keys), in_hbm(values))


def split_kernel(first, tile, w_hbm, high_ref, low_ref, buf, sems):
    chunks = buf.shape[0]
    copies = [
        pltpu.make_async_copy(w_hbm.at[pl.ds(first + c * tile, tile), :], buf.at[c], sems.at[c])
        for c in range(chunks)
    ]
    for copy in copies:
        copy.start()
    for c in range(chunks):
        copies[c].wait()
        rows = slice(c * tile, (c + 1) * tile)
        high_ref[rows, :], low_ref[rows, :] = pieces_of(buf[c], 2)


def split_weight(weight, first, count):
    width = weight.shape[1]
    tile = min(count, 64)
    out = jax.ShapeDtypeStruct((count, width), jnp.bfloat16)
    return pl.pallas_call(
        functools.partial(split_kernel, first, tile),
        out_shape=[out, out],
        in_specs=[IN_PLACE],
        out_specs=[IN_VMEM] * 2,
        scratch_shapes=[
            pltpu.VMEM((count // tile, tile, width), jnp.float32),
            pltpu.SemaphoreType.DMA((count // tile,)),
        ],
        compiler_params=limit(12),
        cost_estimate=pl.CostEstimate(
            flops=8 * count * width, bytes_accessed=8 * count * width, transcendentals=0
        ),
        name="split",
    )(in_hbm(weight))


def attend_kernel(bits, key_count, start, limit_ref, *refs):
    sub = 1 << bits
    q_refs, kv_refs, ref = refs[: -KVH - 1], refs[-KVH - 1 : -1], refs[-1]
    position = lax.axis_index("blk")
    plane, place = position // sub, position % sub
    rows = limit_ref.shape[0]
    per_owner = GROUP // sub
    held = key_count * KVH

    at = lax.broadcasted_iota(jnp.int32, (1, held), 1)
    source = (plane ^ (at // key_count)) * sub + place
    visible = (source * key_count + at % key_count) < limit_ref[:, :1]

    keys = jnp.concatenate([r[:key_count, :] for r in kv_refs], axis=0)
    values = jnp.concatenate([r[key_count:, :] for r in kv_refs], axis=0)
    k1, k2, k3 = pieces_of(keys, 3)
    k12, k31 = jnp.concatenate([k1, k2], axis=1), jnp.concatenate([k3, k1], axis=1)
    v1, v2 = pieces_of(values, 2)
    v12 = jnp.concatenate([v1, v2], axis=1)
    both = (((1,), (1,)), ((), ()))
    scale = 1.0 / math.sqrt(HD)

    half = GROUP // 2
    cross = jnp.broadcast_to(visible[None], (half, rows, held))
    heads = []
    for head in range(start, start + half):
        owner = place ^ reverse_bits(head // per_owner, bits)
        lanes = pl.ds(pl.multiple_of((owner * per_owner + head % per_owner) * HD, HD), HD)
        heads += [q_ref[:, lanes] for q_ref in q_refs]
    q1, q2, q3 = pieces_of(jnp.concatenate(heads, axis=0), 3)
    q11, q22 = jnp.concatenate([q1, q1], axis=1), jnp.concatenate([q2, q2], axis=1)
    q13 = jnp.concatenate([q1, q3], axis=1)
    scores = times(q11, k12, both) + (times(q22, k12, both) + times(q13, k31, both))
    scores = scores.reshape(half, rows, held) * scale
    masked = jnp.where(cross, scores, NEG_FILL)
    peak = jnp.max(masked, axis=2, keepdims=True)
    weights = jnp.where(cross, jnp.exp(masked - peak), 0.0)
    total = jnp.sum(weights, axis=2, keepdims=True)
    w1, w2 = pieces_of(weights.reshape(half * rows, held), 2)
    wide = times(w1, v12)
    sums = wide[:, :HD] + (wide[:, HD:] + times(w2, v1))
    for i in range(half):
        ref[:, i * HD : (i + 1) * HD] = sums[i * rows : (i + 1) * rows]
    stats = [peak[i] for i in range(half)] + [total[i] for i in range(half)]
    ref[:, half * HD :] = lanes_of(stats, rows)


def attend(bits, start, limits, q_parts, kv_held):
    rows, width, key_count = limits.shape[0], GROUP // 2 * HD, kv_held[0].shape[0] // 2
    pairs = rows * GROUP // 2 * key_count * KVH
    return pl.pallas_call(
        functools.partial(attend_kernel, bits, key_count, start),
        out_shape=jax.ShapeDtypeStruct((rows, width + LANES), jnp.float32),
        in_specs=[IN_VMEM] * (1 + len(q_parts) + KVH),
        out_specs=IN_VMEM,
        compiler_params=limit(16),
        cost_estimate=pl.CostEstimate(
            flops=12 * pairs * HD, bytes_accessed=4 * rows * width, transcendentals=pairs
        ),
        name="attend",
    )(limits, *q_parts, *kv_held)


def merged(keep_ref, recv_ref, swap):
    heads = (keep_ref.shape[1] - LANES) // HD
    mine, other = keep_ref[:, heads * HD :], swap_rows(recv_ref[:, heads * HD :], swap)
    sums, peaks, totals = [], [], []
    for i in range(heads):
        peak_a, peak_b = mine[:, i : i + 1], other[:, i : i + 1]
        peak = jnp.maximum(peak_a, peak_b)
        factor_a, factor_b = jnp.exp(peak_a - peak), jnp.exp(peak_b - peak)
        cols = slice(i * HD, (i + 1) * HD)
        sums.append(keep_ref[:, cols] * factor_a + swap_rows(recv_ref[:, cols], swap) * factor_b)
        peaks.append(peak)
        totals.append(
            mine[:, heads + i : heads + i + 1] * factor_a + other[:, heads + i : heads + i + 1] * factor_b
        )
    return sums, peaks, totals


def merge_kernel(swap, keep_ref, recv_ref, send_out, keep_out):
    sums, peaks, totals = merged(keep_ref, recv_ref, swap)
    half = len(sums) // 2
    for start, ref in ((0, keep_out), (half, send_out)):
        for i in range(half):
            ref[:, i * HD : (i + 1) * HD] = sums[start + i]
        stats = peaks[start : start + half] + totals[start : start + half]
        ref[:, half * HD :] = lanes_of(stats, keep_ref.shape[0])


def merge(swap, keep, recv):
    rows, width = keep.shape
    half = (width - LANES) // HD // 2
    out = jax.ShapeDtypeStruct((rows, half * HD + LANES), jnp.float32)
    return pl.pallas_call(
        functools.partial(merge_kernel, swap),
        out_shape=[out, out],
        in_specs=[IN_VMEM] * 2,
        out_specs=[IN_VMEM] * 2,
        compiler_params=limit(4),
        name="merge",
    )(keep, recv)


def project_kernel(swap, tile, keep_ref, recv_ref, *refs):
    piece_refs, (send_out, keep_out) = refs[:-2], refs[-2:]
    sums, _, totals = merged(keep_ref, recv_ref, swap)
    attended = jnp.concatenate([a / t for a, t in zip(sums, totals)], axis=1)
    rows = attended.shape[0]
    half = rows // 2
    a1, a2 = pieces_of(attended, 2)
    a12 = jnp.concatenate([a1, a2], axis=0)
    for c in range(keep_out.shape[1] // tile):
        cols = slice(c * tile, (c + 1) * tile)
        out, first = 0.0, 0
        for high_ref, low_ref in zip(piece_refs[::2], piece_refs[1::2]):
            used = slice(first, first + high_ref.shape[0])
            first = used.stop
            top = times(a12[:, used], high_ref[:, cols])
            out = out + (top[:rows] + (top[rows:] + times(a1[:, used], low_ref[:, cols])))
        keep_out[:, cols] = out[:half]
        send_out[:, cols] = out[half:]


def project(swap, keep, recv, pieces):
    width = pieces[0].shape[1]
    out = jax.ShapeDtypeStruct((keep.shape[0] // 2, width), jnp.float32)
    return pl.pallas_call(
        functools.partial(project_kernel, swap, min(width, 512)),
        out_shape=[out, out],
        in_specs=[IN_VMEM] * (2 + len(pieces)),
        out_specs=[IN_VMEM] * 2,
        compiler_params=limit(16),
        name="project",
    )(keep, recv, *pieces)


def by_planes(bits, queries, keys, values, weight, lengths):
    blocks = lax.axis_size("blk")
    sub = 1 << bits
    local_rows = queries.shape[0]
    part = KVH * local_rows

    def swap(x, mask):
        return lax.ppermute(x, "blk", [(i, i ^ mask) for i in range(blocks)])

    q_send, limits = pack_q(bits, lengths, queries)
    kv_send = pack_kv(bits, keys, values)
    kv_held = [kv_send[0]] + [swap(kv_send[k], k * sub) for k in range(1, KVH)]
    wide = GROUP * HD
    q_rows = [[q] for q in q_send[1:]]
    q_out = q_send[0]
    for b in reversed(range(PLANE_BITS)):
        q_in = swap(q_out, sub << b)
        count = len(q_rows[0])
        got = [q_in[:, i * wide : (i + 1) * wide] for i in range(q_in.shape[1] // wide)]
        q_rows = [rows + got[t * count : (t + 1) * count] for t, rows in enumerate(q_rows)]
        high = q_rows[len(q_rows) // 2 :]
        if b:
            q_out = jnp.concatenate([piece for rows in high for piece in rows], axis=1)
            q_rows = q_rows[: len(q_rows) // 2]
    q_parts = [jnp.concatenate(q_rows[0], axis=0)]
    for b in reversed(range(bits)):
        q_parts = q_parts + [swap(x, 1 << b) for x in q_parts]
    features = weight.shape[0]
    pieces = []
    for i in range(2):
        pieces += split_weight(weight, i * features // 2, features // 2)

    send = attend(bits, GROUP // 2, limits, q_parts, kv_held)
    keep = attend(bits, 0, limits, q_parts, kv_held)
    for b in range(bits - 1):
        send, keep = merge(part << (bits - 1 - b), keep, swap(send, 1 << b))
    send, keep = project(part, keep, swap(send, 1 << (bits - 1)), pieces)

    recv = swap(send, 1)
    for b in range(1, bits):
        half = keep.shape[0] // 2
        send = keep[half:] + recv[half:]
        keep = keep[:half] + recv[:half]
        recv = swap(send, 1 << b)
    total = keep + recv
    out = total[:local_rows]
    for order in range(1, KVH):
        k = relative(order, 0)
        out = out + swap(total[order * local_rows : (order + 1) * local_rows], k * sub)
    return out


def head_partials(query_rows, keys_held, values_held, key_pos, lengths):
    row_count = query_rows.shape[0]
    grouped = query_rows.reshape(row_count, GROUP, HD)
    scores = jnp.einsum(
        "tje,pe->tjp", grouped, keys_held, precision=HIGHEST, preferred_element_type=jnp.float32
    ) * (1.0 / math.sqrt(HD))
    request_ids = jnp.arange(row_count, dtype=jnp.int32) // REQ_TOK
    request_table = jnp.arange(lengths.shape[0], dtype=jnp.int32)
    limits = jnp.sum(
        jnp.where(request_ids[:, None] == request_table[None, :], lengths[None, :], 0), axis=1
    )
    visible = (key_pos[None, :] < limits[:, None])[:, None, :]
    masked = jnp.where(visible, scores, NEG_FILL)
    peak_vals = jnp.max(masked, axis=2)
    weights = jnp.where(visible, jnp.exp(masked - peak_vals[..., None]), 0.0)
    totals = jnp.sum(weights, axis=2)
    mixed_values = jnp.einsum(
        "tjp,pe->tje", weights, values_held, precision=HIGHEST, preferred_element_type=jnp.float32
    )
    return mixed_values.reshape(row_count, GROUP * HD), peak_vals, totals


def by_all_to_all(queries, keys, values, weight, lengths):
    blocks = lax.axis_size("blk")
    position = lax.axis_index("blk")
    local_rows = queries.shape[0]
    total_rows = local_rows * blocks
    key_count = keys.shape[0]
    sub_count = blocks // KVH
    sub_len = key_count // sub_count

    def exchange(x, split, concat):
        return lax.all_to_all(x, "blk", split_axis=split, concat_axis=concat, tiled=True)

    def spread(x):
        split = x.reshape(sub_count, sub_len, KVH, HD).transpose(0, 2, 1, 3)
        return exchange(split.reshape(blocks, sub_len, HD), 0, 0).reshape(blocks * sub_len, HD)

    held_pos = (
        jnp.arange(blocks, dtype=jnp.int32)[:, None] * key_count
        + position // KVH * sub_len
        + jnp.arange(sub_len, dtype=jnp.int32)[None, :]
    ).reshape(blocks * sub_len)
    query_heads = queries.reshape(local_rows, KVH, GROUP * HD).transpose(1, 0, 2)
    query_send = jnp.broadcast_to(query_heads[None], (sub_count, KVH, local_rows, GROUP * HD))
    query_held = exchange(query_send.reshape(blocks, local_rows, GROUP * HD), 0, 0)
    sums, peaks, totals = head_partials(
        query_held.reshape(total_rows, GROUP * HD), spread(keys), spread(values), held_pos, lengths
    )
    sums = exchange(sums, 0, 0).reshape(sub_count, KVH, local_rows, GROUP, HD)
    peaks = exchange(peaks, 0, 0).reshape(sub_count, KVH, local_rows, GROUP)
    totals = exchange(totals, 0, 0).reshape(sub_count, KVH, local_rows, GROUP)
    factor = jnp.exp(peaks - jnp.max(peaks, axis=0)[None])
    numerator = jnp.sum(sums * factor[..., None], axis=0)
    denominator = jnp.sum(totals * factor, axis=0)
    attended = (numerator / denominator[..., None]).transpose(1, 0, 2, 3).reshape(local_rows, H * HD)
    feature_rows = exchange(attended, 1, 0)
    parts = jnp.dot(feature_rows, weight, precision=HIGHEST, preferred_element_type=jnp.float32)
    return jnp.sum(exchange(parts, 0, 0).reshape(blocks, local_rows, weight.shape[1]), axis=0)


def per_device(queries, prefix_keys, prefix_values, out_weight, lengths):
    blocks = lax.axis_size("blk")
    sub = blocks // KVH
    bits = sub.bit_length() - 1
    fits = (
        blocks == KVH << bits
        and bits >= 1
        and GROUP % sub == 0
        and (KVH * queries.shape[0]) % 8 == 0
        and prefix_keys.shape[0] % LANES == 0
    )
    if fits:
        return by_planes(bits, queries, prefix_keys, prefix_values, out_weight, lengths)
    return by_all_to_all(queries, prefix_keys, prefix_values, out_weight, lengths)


def solution(mesh):
    in_specs = (
        P(("groups", "blk"), None),
        P(("groups", "blk"), None),
        P(("groups", "blk"), None),
        P("blk", None),
        P("groups"),
    )
    out_specs = P(("groups", "blk"), None)
    return jax.shard_map(
        per_device, mesh=mesh, in_specs=in_specs, out_specs=out_specs, check_vma=False
    )
```

```python
import functools
import math

import jax
import jax.numpy as jnp
from jax import lax
from jax.experimental import pallas as pl
from jax.experimental.pallas import tpu as pltpu
from jax.sharding import PartitionSpec as P


H = 64
KVH = 4
HD = 128
REQ_TOK = 16
GROUP = H // KVH
PLANE_BITS = KVH.bit_length() - 1
LANES = 128

HIGHEST = lax.Precision.HIGHEST
NEG_FILL = -1e30


VMEM = pltpu.VMEM


def reverse_bits(value, bits):
    out = 0
    for b in range(bits):
        out |= ((value >> b) & 1) << (bits - 1 - b)
    return out


def relative(order, bits):
    out = 0
    for b in range(PLANE_BITS):
        out = out + (((order >> (PLANE_BITS - 1 - b)) & 1) << (bits + b))
    for b in range(bits):
        out = out + (((order >> (PLANE_BITS + bits - 1 - b)) & 1) << b)
    return out


def swap_rows(x, size):
    blocks = [x[i * size : (i + 1) * size] for i in range(x.shape[0] // size)]
    return jnp.concatenate([blocks[i ^ 1] for i in range(len(blocks))], axis=0)


def lanes_of(columns, rows):
    lane = lax.broadcasted_iota(jnp.int32, (rows, LANES), 1)
    out = jnp.zeros((rows, LANES), jnp.float32)
    for i, column in enumerate(columns):
        out = jnp.where(lane == i, column, out)
    return out


def pieces_of(x, count):
    out = []
    for _ in range(count):
        out.append(x.astype(jnp.bfloat16))
        x = x - out[-1].astype(jnp.float32)
    return out


def times(a, b, dims=(((1,), (0,)), ((), ()))):
    return lax.dot_general(a, b, dims, preferred_element_type=jnp.float32)


def limit(mib):
    return pltpu.CompilerParams(vmem_limit_bytes=mib << 20)


IN_VMEM = pl.BlockSpec(memory_space=VMEM)
IN_PLACE = pl.BlockSpec(memory_space=pl.ANY)


def in_hbm(x):
    return pltpu.with_memory_space_constraint(x, pltpu.HBM)


def run_copies(pairs, sems):
    copies = [pltpu.make_async_copy(src, dst, sems.at[i]) for i, (src, dst) in enumerate(pairs)]
    for copy in copies:
        copy.start()
    return copies


def pack_q_kernel(bits, len_hbm, q_hbm, *refs):
    q_outs, (limit_out, len_ref, sems) = refs[:-3], refs[-3:]
    position = lax.axis_index("blk")
    wide, half = GROUP * HD, KVH // 2
    pairs = [(len_hbm, len_ref)]
    for step in reversed(range(KVH)):
        lanes = pl.ds(pl.multiple_of(((position >> bits) ^ step) * wide, wide), wide)
        q_out = q_outs[0].at[:, pl.ds((step - half) * wide, wide)] if step >= half else q_outs[1 + step]
        pairs.append((q_hbm.at[:, lanes], q_out))
    copies = run_copies(pairs, sems)
    local_rows = q_hbm.shape[0]
    row = lax.broadcasted_iota(jnp.int32, limit_out.shape, 0)
    token = (position ^ relative(row // local_rows, bits)) * local_rows + row % local_rows
    request = token // REQ_TOK
    copies[0].wait()
    limits = jnp.zeros(limit_out.shape, jnp.int32)
    for i in range(len_ref.shape[0]):
        limits = jnp.where(request == i, len_ref[i], limits)
    limit_out[...] = limits
    for copy in copies[1:]:
        copy.wait()


def pack_q(bits, lengths, queries):
    local_rows, wide = queries.shape[0], GROUP * HD
    q_high = jax.ShapeDtypeStruct((local_rows, KVH // 2 * wide), jnp.float32)
    q = jax.ShapeDtypeStruct((local_rows, wide), jnp.float32)
    limits = jax.ShapeDtypeStruct(((KVH << bits) * local_rows, LANES), jnp.int32)
    out = pl.pallas_call(
        functools.partial(pack_q_kernel, bits),
        out_shape=[q_high] + [q] * (KVH // 2) + [limits],
        in_specs=[IN_PLACE] * 2,
        out_specs=[IN_VMEM] * (KVH // 2 + 2),
        scratch_shapes=[pltpu.SMEM(lengths.shape, jnp.int32), pltpu.SemaphoreType.DMA((1 + KVH,))],
        compiler_params=limit(4),
        name="pack_q",
    )(in_hbm(lengths), in_hbm(queries))
    return out[:-1], out[-1]


def pack_kv_kernel(bits, k_hbm, v_hbm, *refs):
    kv_outs, sems = refs[:-1], refs[-1]
    plane = lax.axis_index("blk") >> bits
    keys = k_hbm.shape[0]
    pairs = []
    for step in reversed(range(KVH)):
        lanes = pl.ds(pl.multiple_of((plane ^ step) * HD, HD), HD)
        pairs.append((k_hbm.at[:, lanes], kv_outs[step].at[pl.ds(0, keys), :]))
        pairs.append((v_hbm.at[:, lanes], kv_outs[step].at[pl.ds(keys, keys), :]))
    for copy in run_copies(pairs, sems):
        copy.wait()


def pack_kv(bits, keys, values):
    kv = jax.ShapeDtypeStruct((2 * keys.shape[0], HD), jnp.float32)
    return pl.pallas_call(
        functools.partial(pack_kv_kernel, bits),
        out_shape=[kv] * KVH,
        in_specs=[IN_PLACE] * 2,
        out_specs=[IN_VMEM] * KVH,
        scratch_shapes=[pltpu.SemaphoreType.DMA((2 * KVH,))],
        compiler_params=limit(4),
        cost_estimate=pl.CostEstimate(flops=0, bytes_accessed=16 * keys.size, transcendentals=0),
        name="pack_kv",
    )(in_hbm(keys), in_hbm(values))


def split_kernel(first, tile, w_hbm, high_ref, low_ref, buf, sems):
    chunks = buf.shape[0]
    copies = [
        pltpu.make_async_copy(w_hbm.at[pl.ds(first + c * tile, tile), :], buf.at[c], sems.at[c])
        for c in range(chunks)
    ]
    for copy in copies:
        copy.start()
    for c in range(chunks):
        copies[c].wait()
        rows = slice(c * tile, (c + 1) * tile)
        high_ref[rows, :], low_ref[rows, :] = pieces_of(buf[c], 2)


def split_weight(weight, first, count):
    width = weight.shape[1]
    tile = min(count, 64)
    out = jax.ShapeDtypeStruct((count, width), jnp.bfloat16)
    return pl.pallas_call(
        functools.partial(split_kernel, first, tile),
        out_shape=[out, out],
        in_specs=[IN_PLACE],
        out_specs=[IN_VMEM] * 2,
        scratch_shapes=[
            pltpu.VMEM((count // tile, tile, width), jnp.float32),
            pltpu.SemaphoreType.DMA((count // tile,)),
        ],
        compiler_params=limit(12),
        cost_estimate=pl.CostEstimate(
            flops=8 * count * width, bytes_accessed=8 * count * width, transcendentals=0
        ),
        name="split",
    )(in_hbm(weight))


def attend_kernel(bits, key_count, start, limit_ref, *refs):
    sub = 1 << bits
    q_refs, kv_refs, ref = refs[: -KVH - 1], refs[-KVH - 1 : -1], refs[-1]
    position = lax.axis_index("blk")
    plane, place = position // sub, position % sub
    rows = limit_ref.shape[0]
    per_owner = GROUP // sub
    held = key_count * KVH

    at = lax.broadcasted_iota(jnp.int32, (1, held), 1)
    source = (plane ^ (at // key_count)) * sub + place
    visible = (source * key_count + at % key_count) < limit_ref[:, :1]

    keys = jnp.concatenate([r[:key_count, :] for r in kv_refs], axis=0)
    values = jnp.concatenate([r[key_count:, :] for r in kv_refs], axis=0)
    k1, k2, k3 = pieces_of(keys, 3)
    k12, k31 = jnp.concatenate([k1, k2], axis=1), jnp.concatenate([k3, k1], axis=1)
    v1, v2 = pieces_of(values, 2)
    v12 = jnp.concatenate([v1, v2], axis=1)
    both = (((1,), (1,)), ((), ()))
    scale = 1.0 / math.sqrt(HD)

    half = GROUP // 2
    cross = jnp.broadcast_to(visible[None], (half, rows, held))
    heads = []
    for head in range(start, start + half):
        owner = place ^ reverse_bits(head // per_owner, bits)
        lanes = pl.ds(pl.multiple_of((owner * per_owner + head % per_owner) * HD, HD), HD)
        heads += [q_ref[:, lanes] for q_ref in q_refs]
    q1, q2, q3 = pieces_of(jnp.concatenate(heads, axis=0), 3)
    q11, q22 = jnp.concatenate([q1, q1], axis=1), jnp.concatenate([q2, q2], axis=1)
    q13 = jnp.concatenate([q1, q3], axis=1)
    scores = times(q11, k12, both) + (times(q22, k12, both) + times(q13, k31, both))
    scores = scores.reshape(half, rows, held) * scale
    masked = jnp.where(cross, scores, NEG_FILL)
    peak = jnp.max(masked, axis=2, keepdims=True)
    weights = jnp.where(cross, jnp.exp(masked - peak), 0.0)
    total = jnp.sum(weights, axis=2, keepdims=True)
    w1, w2 = pieces_of(weights.reshape(half * rows, held), 2)
    wide = times(w1, v12)
    sums = wide[:, :HD] + (wide[:, HD:] + times(w2, v1))
    for i in range(half):
        ref[:, i * HD : (i + 1) * HD] = sums[i * rows : (i + 1) * rows]
    stats = [peak[i] for i in range(half)] + [total[i] for i in range(half)]
    ref[:, half * HD :] = lanes_of(stats, rows)


def attend(bits, start, limits, q_parts, kv_held):
    rows, width, key_count = limits.shape[0], GROUP // 2 * HD, kv_held[0].shape[0] // 2
    pairs = rows * GROUP // 2 * key_count * KVH
    return pl.pallas_call(
        functools.partial(attend_kernel, bits, key_count, start),
        out_shape=jax.ShapeDtypeStruct((rows, width + LANES), jnp.float32),
        in_specs=[IN_VMEM] * (1 + len(q_parts) + KVH),
        out_specs=IN_VMEM,
        compiler_params=limit(16),
        cost_estimate=pl.CostEstimate(
            flops=12 * pairs * HD, bytes_accessed=4 * rows * width, transcendentals=pairs
        ),
        name="attend",
    )(limits, *q_parts, *kv_held)


def merged(keep_ref, recv_ref, swap):
    heads = (keep_ref.shape[1] - LANES) // HD
    mine, other = keep_ref[:, heads * HD :], swap_rows(recv_ref[:, heads * HD :], swap)
    sums, peaks, totals = [], [], []
    for i in range(heads):
        peak_a, peak_b = mine[:, i : i + 1], other[:, i : i + 1]
        peak = jnp.maximum(peak_a, peak_b)
        factor_a, factor_b = jnp.exp(peak_a - peak), jnp.exp(peak_b - peak)
        cols = slice(i * HD, (i + 1) * HD)
        sums.append(keep_ref[:, cols] * factor_a + swap_rows(recv_ref[:, cols], swap) * factor_b)
        peaks.append(peak)
        totals.append(
            mine[:, heads + i : heads + i + 1] * factor_a + other[:, heads + i : heads + i + 1] * factor_b
        )
    return sums, peaks, totals


def merge_kernel(swap, keep_ref, recv_ref, send_out, keep_out):
    sums, peaks, totals = merged(keep_ref, recv_ref, swap)
    half = len(sums) // 2
    for start, ref in ((0, keep_out), (half, send_out)):
        for i in range(half):
            ref[:, i * HD : (i + 1) * HD] = sums[start + i]
        stats = peaks[start : start + half] + totals[start : start + half]
        ref[:, half * HD :] = lanes_of(stats, keep_ref.shape[0])


def merge(swap, keep, recv):
    rows, width = keep.shape
    half = (width - LANES) // HD // 2
    out = jax.ShapeDtypeStruct((rows, half * HD + LANES), jnp.float32)
    return pl.pallas_call(
        functools.partial(merge_kernel, swap),
        out_shape=[out, out],
        in_specs=[IN_VMEM] * 2,
        out_specs=[IN_VMEM] * 2,
        compiler_params=limit(4),
        name="merge",
    )(keep, recv)


def project_kernel(swap, tile, keep_ref, recv_ref, *refs):
    piece_refs, (send_out, keep_out) = refs[:-2], refs[-2:]
    sums, _, totals = merged(keep_ref, recv_ref, swap)
    attended = jnp.concatenate([a / t for a, t in zip(sums, totals)], axis=1)
    rows = attended.shape[0]
    half = rows // 2
    a1, a2 = pieces_of(attended, 2)
    a12 = jnp.concatenate([a1, a2], axis=0)
    for c in range(keep_out.shape[1] // tile):
        cols = slice(c * tile, (c + 1) * tile)
        out, first = 0.0, 0
        for high_ref, low_ref in zip(piece_refs[::2], piece_refs[1::2]):
            used = slice(first, first + high_ref.shape[0])
            first = used.stop
            top = times(a12[:, used], high_ref[:, cols])
            out = out + (top[:rows] + (top[rows:] + times(a1[:, used], low_ref[:, cols])))
        keep_out[:, cols] = out[:half]
        send_out[:, cols] = out[half:]


def project(swap, keep, recv, pieces):
    width = pieces[0].shape[1]
    out = jax.ShapeDtypeStruct((keep.shape[0] // 2, width), jnp.float32)
    return pl.pallas_call(
        functools.partial(project_kernel, swap, min(width, 512)),
        out_shape=[out, out],
        in_specs=[IN_VMEM] * (2 + len(pieces)),
        out_specs=[IN_VMEM] * 2,
        compiler_params=limit(16),
        name="project",
    )(keep, recv, *pieces)


def by_planes(bits, queries, keys, values, weight, lengths):
    blocks = lax.axis_size("blk")
    sub = 1 << bits
    local_rows = queries.shape[0]
    part = KVH * local_rows

    def swap(x, mask):
        return lax.ppermute(x, "blk", [(i, i ^ mask) for i in range(blocks)])

    q_send, limits = pack_q(bits, lengths, queries)
    kv_send = pack_kv(bits, keys, values)
    kv_held = [kv_send[0]] + [swap(kv_send[k], k * sub) for k in range(1, KVH)]
    wide = GROUP * HD
    q_rows = [[q] for q in q_send[1:]]
    q_out = q_send[0]
    for b in reversed(range(PLANE_BITS)):
        q_in = swap(q_out, sub << b)
        count = len(q_rows[0])
        got = [q_in[:, i * wide : (i + 1) * wide] for i in range(q_in.shape[1] // wide)]
        q_rows = [rows + got[t * count : (t + 1) * count] for t, rows in enumerate(q_rows)]
        high = q_rows[len(q_rows) // 2 :]
        if b:
            q_out = jnp.concatenate([piece for rows in high for piece in rows], axis=1)
            q_rows = q_rows[: len(q_rows) // 2]
    q_parts = [jnp.concatenate(q_rows[0], axis=0)]
    for b in reversed(range(bits)):
        q_parts = q_parts + [swap(x, 1 << b) for x in q_parts]
    features = weight.shape[0]
    pieces = []
    for i in range(2):
        pieces += split_weight(weight, i * features // 2, features // 2)

    send = attend(bits, GROUP // 2, limits, q_parts, kv_held)
    keep = attend(bits, 0, limits, q_parts, kv_held)
    for b in range(bits - 1):
        send, keep = merge(part << (bits - 1 - b), keep, swap(send, 1 << b))
    send, keep = project(part, keep, swap(send, 1 << (bits - 1)), pieces)

    recv = swap(send, 1)
    quarter = keep.shape[0] // 4
    rows = [slice(i * quarter, (i + 1) * quarter) for i in range(4)]
    total = keep[rows[0]] + recv[rows[0]]
    for i, mask in ((1, sub), (2, 2), (3, 2 + sub)):
        total = total + swap(keep[rows[i]] + recv[rows[i]], mask)
    out = total[:local_rows] + swap(total[local_rows:], 2 * sub)
    return out


def head_partials(query_rows, keys_held, values_held, key_pos, lengths):
    row_count = query_rows.shape[0]
    grouped = query_rows.reshape(row_count, GROUP, HD)
    scores = jnp.einsum(
        "tje,pe->tjp", grouped, keys_held, precision=HIGHEST, preferred_element_type=jnp.float32
    ) * (1.0 / math.sqrt(HD))
    request_ids = jnp.arange(row_count, dtype=jnp.int32) // REQ_TOK
    request_table = jnp.arange(lengths.shape[0], dtype=jnp.int32)
    limits = jnp.sum(
        jnp.where(request_ids[:, None] == request_table[None, :], lengths[None, :], 0), axis=1
    )
    visible = (key_pos[None, :] < limits[:, None])[:, None, :]
    masked = jnp.where(visible, scores, NEG_FILL)
    peak_vals = jnp.max(masked, axis=2)
    weights = jnp.where(visible, jnp.exp(masked - peak_vals[..., None]), 0.0)
    totals = jnp.sum(weights, axis=2)
    mixed_values = jnp.einsum(
        "tjp,pe->tje", weights, values_held, precision=HIGHEST, preferred_element_type=jnp.float32
    )
    return mixed_values.reshape(row_count, GROUP * HD), peak_vals, totals


def by_all_to_all(queries, keys, values, weight, lengths):
    blocks = lax.axis_size("blk")
    position = lax.axis_index("blk")
    local_rows = queries.shape[0]
    total_rows = local_rows * blocks
    key_count = keys.shape[0]
    sub_count = blocks // KVH
    sub_len = key_count // sub_count

    def exchange(x, split, concat):
        return lax.all_to_all(x, "blk", split_axis=split, concat_axis=concat, tiled=True)

    def spread(x):
        split = x.reshape(sub_count, sub_len, KVH, HD).transpose(0, 2, 1, 3)
        return exchange(split.reshape(blocks, sub_len, HD), 0, 0).reshape(blocks * sub_len, HD)

    held_pos = (
        jnp.arange(blocks, dtype=jnp.int32)[:, None] * key_count
        + position // KVH * sub_len
        + jnp.arange(sub_len, dtype=jnp.int32)[None, :]
    ).reshape(blocks * sub_len)
    query_heads = queries.reshape(local_rows, KVH, GROUP * HD).transpose(1, 0, 2)
    query_send = jnp.broadcast_to(query_heads[None], (sub_count, KVH, local_rows, GROUP * HD))
    query_held = exchange(query_send.reshape(blocks, local_rows, GROUP * HD), 0, 0)
    sums, peaks, totals = head_partials(
        query_held.reshape(total_rows, GROUP * HD), spread(keys), spread(values), held_pos, lengths
    )
    sums = exchange(sums, 0, 0).reshape(sub_count, KVH, local_rows, GROUP, HD)
    peaks = exchange(peaks, 0, 0).reshape(sub_count, KVH, local_rows, GROUP)
    totals = exchange(totals, 0, 0).reshape(sub_count, KVH, local_rows, GROUP)
    factor = jnp.exp(peaks - jnp.max(peaks, axis=0)[None])
    numerator = jnp.sum(sums * factor[..., None], axis=0)
    denominator = jnp.sum(totals * factor, axis=0)
    attended = (numerator / denominator[..., None]).transpose(1, 0, 2, 3).reshape(local_rows, H * HD)
    feature_rows = exchange(attended, 1, 0)
    parts = jnp.dot(feature_rows, weight, precision=HIGHEST, preferred_element_type=jnp.float32)
    return jnp.sum(exchange(parts, 0, 0).reshape(blocks, local_rows, weight.shape[1]), axis=0)


def per_device(queries, prefix_keys, prefix_values, out_weight, lengths):
    blocks = lax.axis_size("blk")
    sub = blocks // KVH
    bits = sub.bit_length() - 1
    fits = (
        blocks == KVH << bits
        and bits >= 1
        and GROUP % sub == 0
        and (KVH * queries.shape[0]) % 8 == 0
        and prefix_keys.shape[0] % LANES == 0
    )
    if fits:
        return by_planes(bits, queries, prefix_keys, prefix_values, out_weight, lengths)
    return by_all_to_all(queries, prefix_keys, prefix_values, out_weight, lengths)


def solution(mesh):
    in_specs = (
        P(("groups", "blk"), None),
        P(("groups", "blk"), None),
        P(("groups", "blk"), None),
        P("blk", None),
        P("groups"),
    )
    out_specs = P(("groups", "blk"), None)
    return jax.shard_map(
        per_device, mesh=mesh, in_specs=in_specs, out_specs=out_specs, check_vma=False
    )
```

```python
import functools
import math

import jax
import jax.numpy as jnp
from jax import lax
from jax.experimental import pallas as pl
from jax.experimental.pallas import tpu as pltpu
from jax.sharding import PartitionSpec as P


H = 64
KVH = 4
HD = 128
REQ_TOK = 16
GROUP = H // KVH
PLANE_BITS = KVH.bit_length() - 1
LANES = 128

HIGHEST = lax.Precision.HIGHEST
NEG_FILL = -1e30


VMEM = pltpu.VMEM


def relative(order, bits):
    out = 0
    for b in range(PLANE_BITS):
        out = out + (((order >> (PLANE_BITS - 1 - b)) & 1) << (bits + b))
    for b in range(bits):
        out = out + (((order >> (PLANE_BITS + bits - 1 - b)) & 1) << b)
    return out


def swap_rows(x, size):
    blocks = [x[i * size : (i + 1) * size] for i in range(x.shape[0] // size)]
    return jnp.concatenate([blocks[i ^ 1] for i in range(len(blocks))], axis=0)


def lanes_of(columns, rows):
    lane = lax.broadcasted_iota(jnp.int32, (rows, LANES), 1)
    out = jnp.zeros((rows, LANES), jnp.float32)
    for i, column in enumerate(columns):
        out = jnp.where(lane == i, column, out)
    return out


def pieces_of(x, count):
    out = []
    for _ in range(count):
        out.append(x.astype(jnp.bfloat16))
        x = x - out[-1].astype(jnp.float32)
    return out


def times(a, b, dims=(((1,), (0,)), ((), ()))):
    return lax.dot_general(a, b, dims, preferred_element_type=jnp.float32)


def limit(mib):
    return pltpu.CompilerParams(vmem_limit_bytes=mib << 20)


IN_VMEM = pl.BlockSpec(memory_space=VMEM)
IN_PLACE = pl.BlockSpec(memory_space=pl.ANY)


def in_hbm(x):
    return pltpu.with_memory_space_constraint(x, pltpu.HBM)


def run_copies(pairs, sems):
    copies = [pltpu.make_async_copy(src, dst, sems.at[i]) for i, (src, dst) in enumerate(pairs)]
    for copy in copies:
        copy.start()
    return copies


def pack_q_kernel(bits, len_hbm, q_hbm, *refs):
    q_outs, (limit_out, len_ref, sems) = refs[:-3], refs[-3:]
    position = lax.axis_index("blk")
    wide, half = GROUP * HD, KVH // 2
    pairs = [(len_hbm, len_ref)]
    for step in reversed(range(KVH)):
        lanes = pl.ds(pl.multiple_of(((position >> bits) ^ step) * wide, wide), wide)
        q_out = q_outs[0].at[:, pl.ds((step - half) * wide, wide)] if step >= half else q_outs[1 + step]
        pairs.append((q_hbm.at[:, lanes], q_out))
    copies = run_copies(pairs, sems)
    local_rows = q_hbm.shape[0]
    row = lax.broadcasted_iota(jnp.int32, limit_out.shape, 0)
    token = (position ^ relative(row // local_rows, bits)) * local_rows + row % local_rows
    request = token // REQ_TOK
    copies[0].wait()
    limits = jnp.zeros(limit_out.shape, jnp.int32)
    for i in range(len_ref.shape[0]):
        limits = jnp.where(request == i, len_ref[i], limits)
    limit_out[...] = limits
    for copy in copies[1:]:
        copy.wait()


def pack_q(bits, lengths, queries):
    local_rows, wide = queries.shape[0], GROUP * HD
    q_high = jax.ShapeDtypeStruct((local_rows, KVH // 2 * wide), jnp.float32)
    q = jax.ShapeDtypeStruct((local_rows, wide), jnp.float32)
    limits = jax.ShapeDtypeStruct(((KVH << bits) * local_rows, LANES), jnp.int32)
    out = pl.pallas_call(
        functools.partial(pack_q_kernel, bits),
        out_shape=[q_high] + [q] * (KVH // 2) + [limits],
        in_specs=[IN_PLACE] * 2,
        out_specs=[IN_VMEM] * (KVH // 2 + 2),
        scratch_shapes=[pltpu.SMEM(lengths.shape, jnp.int32), pltpu.SemaphoreType.DMA((1 + KVH,))],
        compiler_params=limit(4),
        name="pack_q",
    )(in_hbm(lengths), in_hbm(queries))
    return out[:-1], out[-1]


def pack_kv_kernel(bits, k_hbm, v_hbm, *refs):
    kv_outs, sems = refs[:-1], refs[-1]
    plane = lax.axis_index("blk") >> bits
    keys = k_hbm.shape[0]
    pairs = []
    for step in reversed(range(KVH)):
        lanes = pl.ds(pl.multiple_of((plane ^ step) * HD, HD), HD)
        pairs.append((k_hbm.at[:, lanes], kv_outs[step].at[pl.ds(0, keys), :]))
        pairs.append((v_hbm.at[:, lanes], kv_outs[step].at[pl.ds(keys, keys), :]))
    for copy in run_copies(pairs, sems):
        copy.wait()


def pack_kv(bits, keys, values):
    kv = jax.ShapeDtypeStruct((2 * keys.shape[0], HD), jnp.float32)
    return pl.pallas_call(
        functools.partial(pack_kv_kernel, bits),
        out_shape=[kv] * KVH,
        in_specs=[IN_PLACE] * 2,
        out_specs=[IN_VMEM] * KVH,
        scratch_shapes=[pltpu.SemaphoreType.DMA((2 * KVH,))],
        compiler_params=limit(4),
        cost_estimate=pl.CostEstimate(flops=0, bytes_accessed=16 * keys.size, transcendentals=0),
        name="pack_kv",
    )(in_hbm(keys), in_hbm(values))


def split_kernel(first, tile, w_hbm, high_ref, low_ref, buf, sems):
    chunks = buf.shape[0]
    copies = [
        pltpu.make_async_copy(w_hbm.at[pl.ds(first + c * tile, tile), :], buf.at[c], sems.at[c])
        for c in range(chunks)
    ]
    for copy in copies:
        copy.start()
    for c in range(chunks):
        copies[c].wait()
        rows = slice(c * tile, (c + 1) * tile)
        high_ref[rows, :], low_ref[rows, :] = pieces_of(buf[c], 2)


def split_weight(weight, first, count):
    width = weight.shape[1]
    tile = min(count, 64)
    out = jax.ShapeDtypeStruct((count, width), jnp.bfloat16)
    return pl.pallas_call(
        functools.partial(split_kernel, first, tile),
        out_shape=[out, out],
        in_specs=[IN_PLACE],
        out_specs=[IN_VMEM] * 2,
        scratch_shapes=[
            pltpu.VMEM((count // tile, tile, width), jnp.float32),
            pltpu.SemaphoreType.DMA((count // tile,)),
        ],
        compiler_params=limit(12),
        cost_estimate=pl.CostEstimate(
            flops=8 * count * width, bytes_accessed=8 * count * width, transcendentals=0
        ),
        name="split",
    )(in_hbm(weight))


def attend_kernel(bits, key_count, rels, limit_ref, *refs):
    sub = 1 << bits
    inputs, outs = refs[: -len(rels)], refs[-len(rels) :]
    q_refs, kv_refs = inputs[:-KVH], inputs[-KVH:]
    position = lax.axis_index("blk")
    plane, place = position // sub, position % sub
    rows = limit_ref.shape[0]
    per_owner = GROUP // sub
    held = key_count * KVH

    at = lax.broadcasted_iota(jnp.int32, (1, held), 1)
    source = (plane ^ (at // key_count)) * sub + place
    visible = (source * key_count + at % key_count) < limit_ref[:, :1]

    keys = jnp.concatenate([r[:key_count, :] for r in kv_refs], axis=0)
    values = jnp.concatenate([r[key_count:, :] for r in kv_refs], axis=0)
    k1, k2, k3 = pieces_of(keys, 3)
    k12, k31 = jnp.concatenate([k1, k2], axis=1), jnp.concatenate([k3, k1], axis=1)
    v1, v2 = pieces_of(values, 2)
    v12 = jnp.concatenate([v1, v2], axis=1)
    both = (((1,), (1,)), ((), ()))
    scale = 1.0 / math.sqrt(HD)

    count = len(rels) * per_owner
    cross = jnp.broadcast_to(visible[None], (count, rows, held))
    heads = []
    for rel in rels:
        for i in range(per_owner):
            lanes = pl.ds(pl.multiple_of(((place ^ rel) * per_owner + i) * HD, HD), HD)
            heads += [q_ref[:, lanes] for q_ref in q_refs]
    q1, q2, q3 = pieces_of(jnp.concatenate(heads, axis=0), 3)
    q11, q22 = jnp.concatenate([q1, q1], axis=1), jnp.concatenate([q2, q2], axis=1)
    q13 = jnp.concatenate([q1, q3], axis=1)
    scores = times(q11, k12, both) + (times(q22, k12, both) + times(q13, k31, both))
    scores = scores.reshape(count, rows, held) * scale
    masked = jnp.where(cross, scores, NEG_FILL)
    peak = jnp.max(masked, axis=2, keepdims=True)
    weights = jnp.where(cross, jnp.exp(masked - peak), 0.0)
    total = jnp.sum(weights, axis=2, keepdims=True)
    w1, w2 = pieces_of(weights.reshape(count * rows, held), 2)
    wide = times(w1, v12)
    sums = wide[:, :HD] + (wide[:, HD:] + times(w2, v1))
    for n, ref in enumerate(outs):
        own = range(n * per_owner, (n + 1) * per_owner)
        for i, head in enumerate(own):
            ref[:, i * HD : (i + 1) * HD] = sums[head * rows : (head + 1) * rows]
        ref[:, per_owner * HD :] = lanes_of([peak[h] for h in own] + [total[h] for h in own], rows)


def attend(bits, rels, limits, q_parts, kv_held):
    rows, key_count = limits.shape[0], kv_held[0].shape[0] // 2
    width = (GROUP >> bits) * HD
    pairs = rows * (GROUP >> bits) * len(rels) * key_count * KVH
    return pl.pallas_call(
        functools.partial(attend_kernel, bits, key_count, rels),
        out_shape=[jax.ShapeDtypeStruct((rows, width + LANES), jnp.float32)] * len(rels),
        in_specs=[IN_VMEM] * (1 + len(q_parts) + KVH),
        out_specs=[IN_VMEM] * len(rels),
        compiler_params=limit(16),
        cost_estimate=pl.CostEstimate(
            flops=12 * pairs * HD, bytes_accessed=4 * rows * width, transcendentals=pairs
        ),
        name="attend",
    )(limits, *q_parts, *kv_held)


def merged(parts):
    heads = (parts[0][0].shape[1] - LANES) // HD

    def read(ref, sizes, cols):
        return functools.reduce(swap_rows, sizes, ref[:, cols])

    stats = [read(ref, sizes, slice(heads * HD, None)) for ref, sizes in parts]
    sums, totals = [], []
    for i in range(heads):
        peaks = [stat[:, i : i + 1] for stat in stats]
        peak = functools.reduce(jnp.maximum, peaks)
        factors = [jnp.exp(x - peak) for x in peaks]
        cols = slice(i * HD, (i + 1) * HD)
        sums.append(sum(read(*part, cols) * f for part, f in zip(parts, factors)))
        at = slice(heads + i, heads + i + 1)
        totals.append(sum(stat[:, at] * f for stat, f in zip(stats, factors)))
    return sums, totals


def project_kernel(swaps, tile, *refs):
    parts, refs = list(zip(refs[: len(swaps)], swaps)), refs[len(swaps) :]
    piece_refs, (send_out, keep_out) = refs[:-2], refs[-2:]
    sums, totals = merged(parts)
    attended = jnp.concatenate([a / t for a, t in zip(sums, totals)], axis=1)
    rows = attended.shape[0]
    half = rows // 2
    a1, a2 = pieces_of(attended, 2)
    a12 = jnp.concatenate([a1, a2], axis=0)
    for c in range(keep_out.shape[1] // tile):
        cols = slice(c * tile, (c + 1) * tile)
        out, first = 0.0, 0
        for high_ref, low_ref in zip(piece_refs[::2], piece_refs[1::2]):
            used = slice(first, first + high_ref.shape[0])
            first = used.stop
            top = times(a12[:, used], high_ref[:, cols])
            out = out + (top[:rows] + (top[rows:] + times(a1[:, used], low_ref[:, cols])))
        keep_out[:, cols] = out[:half]
        send_out[:, cols] = out[half:]


def project(swaps, parts, pieces):
    width = pieces[0].shape[1]
    out = jax.ShapeDtypeStruct((parts[0].shape[0] // 2, width), jnp.float32)
    return pl.pallas_call(
        functools.partial(project_kernel, swaps, min(width, 512)),
        out_shape=[out, out],
        in_specs=[IN_VMEM] * (len(parts) + len(pieces)),
        out_specs=[IN_VMEM] * 2,
        compiler_params=limit(16),
        name="project",
    )(*parts, *pieces)


def by_planes(bits, queries, keys, values, weight, lengths):
    blocks = lax.axis_size("blk")
    sub = 1 << bits
    local_rows = queries.shape[0]
    part = KVH * local_rows

    def swap(x, mask):
        return lax.ppermute(x, "blk", [(i, i ^ mask) for i in range(blocks)])

    q_send, limits = pack_q(bits, lengths, queries)
    kv_send = pack_kv(bits, keys, values)
    kv_held = [kv_send[0]] + [swap(kv_send[k], k * sub) for k in range(1, KVH)]
    wide = GROUP * HD
    q_rows = [[q] for q in q_send[1:]]
    q_out = q_send[0]
    for b in reversed(range(PLANE_BITS)):
        q_in = swap(q_out, sub << b)
        count = len(q_rows[0])
        got = [q_in[:, i * wide : (i + 1) * wide] for i in range(q_in.shape[1] // wide)]
        q_rows = [rows + got[t * count : (t + 1) * count] for t, rows in enumerate(q_rows)]
        high = q_rows[len(q_rows) // 2 :]
        if b:
            q_out = jnp.concatenate([piece for rows in high for piece in rows], axis=1)
            q_rows = q_rows[: len(q_rows) // 2]
    q_parts = [jnp.concatenate(q_rows[0], axis=0)]
    for b in reversed(range(bits)):
        q_parts = q_parts + [swap(x, 1 << b) for x in q_parts]
    features = weight.shape[0]
    pieces = []
    for i in range(2):
        pieces += split_weight(weight, i * features // 2, features // 2)

    core, side = part << 1, part
    far = attend(bits, (3, 2), limits, q_parts, kv_held)
    near = attend(bits, (1, 0), limits, q_parts, kv_held)
    partials = [near[1], swap(near[0], 1), swap(far[1], 2), swap(far[0], 3)]
    send, keep = project(((), (core,), (side,), (core, side)), partials, pieces)

    recv = swap(send, 1)
    quarter = keep.shape[0] // 4
    rows = [slice(i * quarter, (i + 1) * quarter) for i in range(4)]
    total = keep[rows[0]] + recv[rows[0]]
    for i, mask in ((1, sub), (2, 2), (3, 2 + sub)):
        total = total + swap(keep[rows[i]] + recv[rows[i]], mask)
    out = total[:local_rows] + swap(total[local_rows:], 2 * sub)
    return out


def head_partials(query_rows, keys_held, values_held, key_pos, lengths):
    row_count = query_rows.shape[0]
    grouped = query_rows.reshape(row_count, GROUP, HD)
    scores = jnp.einsum(
        "tje,pe->tjp", grouped, keys_held, precision=HIGHEST, preferred_element_type=jnp.float32
    ) * (1.0 / math.sqrt(HD))
    request_ids = jnp.arange(row_count, dtype=jnp.int32) // REQ_TOK
    request_table = jnp.arange(lengths.shape[0], dtype=jnp.int32)
    limits = jnp.sum(
        jnp.where(request_ids[:, None] == request_table[None, :], lengths[None, :], 0), axis=1
    )
    visible = (key_pos[None, :] < limits[:, None])[:, None, :]
    masked = jnp.where(visible, scores, NEG_FILL)
    peak_vals = jnp.max(masked, axis=2)
    weights = jnp.where(visible, jnp.exp(masked - peak_vals[..., None]), 0.0)
    totals = jnp.sum(weights, axis=2)
    mixed_values = jnp.einsum(
        "tjp,pe->tje", weights, values_held, precision=HIGHEST, preferred_element_type=jnp.float32
    )
    return mixed_values.reshape(row_count, GROUP * HD), peak_vals, totals


def by_all_to_all(queries, keys, values, weight, lengths):
    blocks = lax.axis_size("blk")
    position = lax.axis_index("blk")
    local_rows = queries.shape[0]
    total_rows = local_rows * blocks
    key_count = keys.shape[0]
    sub_count = blocks // KVH
    sub_len = key_count // sub_count

    def exchange(x, split, concat):
        return lax.all_to_all(x, "blk", split_axis=split, concat_axis=concat, tiled=True)

    def spread(x):
        split = x.reshape(sub_count, sub_len, KVH, HD).transpose(0, 2, 1, 3)
        return exchange(split.reshape(blocks, sub_len, HD), 0, 0).reshape(blocks * sub_len, HD)

    held_pos = (
        jnp.arange(blocks, dtype=jnp.int32)[:, None] * key_count
        + position // KVH * sub_len
        + jnp.arange(sub_len, dtype=jnp.int32)[None, :]
    ).reshape(blocks * sub_len)
    query_heads = queries.reshape(local_rows, KVH, GROUP * HD).transpose(1, 0, 2)
    query_send = jnp.broadcast_to(query_heads[None], (sub_count, KVH, local_rows, GROUP * HD))
    query_held = exchange(query_send.reshape(blocks, local_rows, GROUP * HD), 0, 0)
    sums, peaks, totals = head_partials(
        query_held.reshape(total_rows, GROUP * HD), spread(keys), spread(values), held_pos, lengths
    )
    sums = exchange(sums, 0, 0).reshape(sub_count, KVH, local_rows, GROUP, HD)
    peaks = exchange(peaks, 0, 0).reshape(sub_count, KVH, local_rows, GROUP)
    totals = exchange(totals, 0, 0).reshape(sub_count, KVH, local_rows, GROUP)
    factor = jnp.exp(peaks - jnp.max(peaks, axis=0)[None])
    numerator = jnp.sum(sums * factor[..., None], axis=0)
    denominator = jnp.sum(totals * factor, axis=0)
    attended = (numerator / denominator[..., None]).transpose(1, 0, 2, 3).reshape(local_rows, H * HD)
    feature_rows = exchange(attended, 1, 0)
    parts = jnp.dot(feature_rows, weight, precision=HIGHEST, preferred_element_type=jnp.float32)
    return jnp.sum(exchange(parts, 0, 0).reshape(blocks, local_rows, weight.shape[1]), axis=0)


def per_device(queries, prefix_keys, prefix_values, out_weight, lengths):
    blocks = lax.axis_size("blk")
    sub = blocks // KVH
    bits = sub.bit_length() - 1
    fits = (
        blocks == KVH << bits
        and bits == 2
        and PLANE_BITS == 2
        and (KVH * queries.shape[0]) % 8 == 0
        and prefix_keys.shape[0] % LANES == 0
    )
    if fits:
        return by_planes(bits, queries, prefix_keys, prefix_values, out_weight, lengths)
    return by_all_to_all(queries, prefix_keys, prefix_values, out_weight, lengths)


def solution(mesh):
    in_specs = (
        P(("groups", "blk"), None),
        P(("groups", "blk"), None),
        P(("groups", "blk"), None),
        P("blk", None),
        P("groups"),
    )
    out_specs = P(("groups", "blk"), None)
    return jax.shard_map(
        per_device, mesh=mesh, in_specs=in_specs, out_specs=out_specs, check_vma=False
    )
```

```python
import functools
import math

import jax
import jax.numpy as jnp
from jax import lax
from jax.experimental import pallas as pl
from jax.experimental.pallas import tpu as pltpu
from jax.sharding import PartitionSpec as P


H = 64
KVH = 4
HD = 128
REQ_TOK = 16
GROUP = H // KVH
PLANE_BITS = KVH.bit_length() - 1
LANES = 128

HIGHEST = lax.Precision.HIGHEST
NEG_FILL = -1e30


VMEM = pltpu.VMEM


def relative(order, bits):
    out = 0
    for b in range(PLANE_BITS):
        out = out + (((order >> (PLANE_BITS - 1 - b)) & 1) << (bits + b))
    for b in range(bits):
        out = out + (((order >> (PLANE_BITS + bits - 1 - b)) & 1) << b)
    return out


def swap_rows(x, size):
    blocks = [x[i * size : (i + 1) * size] for i in range(x.shape[0] // size)]
    return jnp.concatenate([blocks[i ^ 1] for i in range(len(blocks))], axis=0)


def stats_tile(columns, rows):
    lane = lax.broadcasted_iota(jnp.int32, (8, LANES), 1)
    out = jnp.zeros((8, LANES), jnp.float32)
    for g in range(rows // 8):
        for i, column in enumerate(columns):
            out = jnp.where(lane == g * len(columns) + i, column[8 * g : 8 * g + 8], out)
    return out


def stats_column(tile, i, count, rows):
    return jnp.concatenate([tile[:, g * count + i :][:, :1] for g in range(rows // 8)], axis=0)


def pieces_of(x, count):
    out = []
    for _ in range(count):
        out.append(x.astype(jnp.bfloat16))
        x = x - out[-1].astype(jnp.float32)
    return out


def times(a, b, dims=(((1,), (0,)), ((), ()))):
    return lax.dot_general(a, b, dims, preferred_element_type=jnp.float32)


def limit(mib):
    return pltpu.CompilerParams(vmem_limit_bytes=mib << 20)


IN_VMEM = pl.BlockSpec(memory_space=VMEM)
IN_PLACE = pl.BlockSpec(memory_space=pl.ANY)


def in_hbm(x):
    return pltpu.with_memory_space_constraint(x, pltpu.HBM)


def run_copies(pairs, sems):
    copies = [pltpu.make_async_copy(src, dst, sems.at[i]) for i, (src, dst) in enumerate(pairs)]
    for copy in copies:
        copy.start()
    return copies


def pack_q_kernel(bits, len_hbm, q_hbm, *refs):
    q_outs, (limit_out, len_ref, sems) = refs[:-3], refs[-3:]
    position = lax.axis_index("blk")
    wide, half = GROUP * HD, KVH // 2
    pairs = [(len_hbm, len_ref)]
    for step in reversed(range(KVH)):
        lanes = pl.ds(pl.multiple_of(((position >> bits) ^ step) * wide, wide), wide)
        q_out = q_outs[0].at[:, pl.ds((step - half) * wide, wide)] if step >= half else q_outs[1 + step]
        pairs.append((q_hbm.at[:, lanes], q_out))
    copies = run_copies(pairs, sems)
    local_rows = q_hbm.shape[0]
    row = lax.broadcasted_iota(jnp.int32, limit_out.shape, 0)
    token = (position ^ relative(row // local_rows, bits)) * local_rows + row % local_rows
    request = token // REQ_TOK
    copies[0].wait()
    limits = jnp.zeros(limit_out.shape, jnp.int32)
    for i in range(len_ref.shape[0]):
        limits = jnp.where(request == i, len_ref[i], limits)
    limit_out[...] = limits
    for copy in copies[1:]:
        copy.wait()


def pack_q(bits, lengths, queries):
    local_rows, wide = queries.shape[0], GROUP * HD
    q_high = jax.ShapeDtypeStruct((local_rows, KVH // 2 * wide), jnp.float32)
    q = jax.ShapeDtypeStruct((local_rows, wide), jnp.float32)
    limits = jax.ShapeDtypeStruct(((KVH << bits) * local_rows, LANES), jnp.int32)
    out = pl.pallas_call(
        functools.partial(pack_q_kernel, bits),
        out_shape=[q_high] + [q] * (KVH // 2) + [limits],
        in_specs=[IN_PLACE] * 2,
        out_specs=[IN_VMEM] * (KVH // 2 + 2),
        scratch_shapes=[pltpu.SMEM(lengths.shape, jnp.int32), pltpu.SemaphoreType.DMA((1 + KVH,))],
        compiler_params=limit(4),
        name="pack_q",
    )(in_hbm(lengths), in_hbm(queries))
    return out[:-1], out[-1]


def pack_kv_kernel(bits, k_hbm, v_hbm, *refs):
    kv_outs, sems = refs[:-1], refs[-1]
    plane = lax.axis_index("blk") >> bits
    keys = k_hbm.shape[0]
    pairs = []
    for step in reversed(range(KVH)):
        lanes = pl.ds(pl.multiple_of((plane ^ step) * HD, HD), HD)
        pairs.append((k_hbm.at[:, lanes], kv_outs[step].at[pl.ds(0, keys), :]))
        pairs.append((v_hbm.at[:, lanes], kv_outs[step].at[pl.ds(keys, keys), :]))
    for copy in run_copies(pairs, sems):
        copy.wait()


def pack_kv(bits, keys, values):
    kv = jax.ShapeDtypeStruct((2 * keys.shape[0], HD), jnp.float32)
    return pl.pallas_call(
        functools.partial(pack_kv_kernel, bits),
        out_shape=[kv] * KVH,
        in_specs=[IN_PLACE] * 2,
        out_specs=[IN_VMEM] * KVH,
        scratch_shapes=[pltpu.SemaphoreType.DMA((2 * KVH,))],
        compiler_params=limit(4),
        cost_estimate=pl.CostEstimate(flops=0, bytes_accessed=16 * keys.size, transcendentals=0),
        name="pack_kv",
    )(in_hbm(keys), in_hbm(values))


def split_kernel(first, tile, w_hbm, high_ref, low_ref, buf, sems):
    chunks = buf.shape[0]
    copies = [
        pltpu.make_async_copy(w_hbm.at[pl.ds(first + c * tile, tile), :], buf.at[c], sems.at[c])
        for c in range(chunks)
    ]
    for copy in copies:
        copy.start()
    for c in range(chunks):
        copies[c].wait()
        rows = slice(c * tile, (c + 1) * tile)
        high_ref[rows, :], low_ref[rows, :] = pieces_of(buf[c], 2)


def split_weight(weight, first, count):
    width = weight.shape[1]
    tile = min(count, 64)
    out = jax.ShapeDtypeStruct((count, width), jnp.bfloat16)
    return pl.pallas_call(
        functools.partial(split_kernel, first, tile),
        out_shape=[out, out],
        in_specs=[IN_PLACE],
        out_specs=[IN_VMEM] * 2,
        scratch_shapes=[
            pltpu.VMEM((count // tile, tile, width), jnp.float32),
            pltpu.SemaphoreType.DMA((count // tile,)),
        ],
        compiler_params=limit(12),
        cost_estimate=pl.CostEstimate(
            flops=8 * count * width, bytes_accessed=8 * count * width, transcendentals=0
        ),
        name="split",
    )(in_hbm(weight))


def attend_kernel(bits, key_count, rels, limit_ref, *refs):
    sub = 1 << bits
    inputs, outs = refs[: -len(rels)], refs[-len(rels) :]
    q_refs, kv_refs = inputs[:-KVH], inputs[-KVH:]
    position = lax.axis_index("blk")
    plane, place = position // sub, position % sub
    rows = limit_ref.shape[0]
    per_owner = GROUP // sub
    held = key_count * KVH

    at = lax.broadcasted_iota(jnp.int32, (1, held), 1)
    source = (plane ^ (at // key_count)) * sub + place
    visible = (source * key_count + at % key_count) < limit_ref[:, :1]

    keys = jnp.concatenate([r[:key_count, :] for r in kv_refs], axis=0)
    values = jnp.concatenate([r[key_count:, :] for r in kv_refs], axis=0)
    k1, k2, k3 = pieces_of(keys, 3)
    k12, k31 = jnp.concatenate([k1, k2], axis=1), jnp.concatenate([k3, k1], axis=1)
    v1, v2 = pieces_of(values, 2)
    v12 = jnp.concatenate([v1, v2], axis=1)
    both = (((1,), (1,)), ((), ()))
    scale = 1.0 / math.sqrt(HD)

    count = len(rels) * per_owner
    cross = jnp.broadcast_to(visible[None], (count, rows, held))
    heads = []
    for rel in rels:
        for i in range(per_owner):
            lanes = pl.ds(pl.multiple_of(((place ^ rel) * per_owner + i) * HD, HD), HD)
            heads += [q_ref[:, lanes] for q_ref in q_refs]
    q1, q2, q3 = pieces_of(jnp.concatenate(heads, axis=0), 3)
    q11, q22 = jnp.concatenate([q1, q1], axis=1), jnp.concatenate([q2, q2], axis=1)
    q13 = jnp.concatenate([q1, q3], axis=1)
    scores = times(q11, k12, both) + (times(q22, k12, both) + times(q13, k31, both))
    scores = scores.reshape(count, rows, held) * scale
    masked = jnp.where(cross, scores, NEG_FILL)
    peak = jnp.max(masked, axis=2, keepdims=True)
    weights = jnp.where(cross, jnp.exp(masked - peak), 0.0)
    total = jnp.sum(weights, axis=2, keepdims=True)
    w1, w2 = pieces_of(weights.reshape(count * rows, held), 2)
    wide = times(w1, v12)
    sums = wide[:, :HD] + (wide[:, HD:] + times(w2, v1))
    for n, ref in enumerate(outs):
        own = range(n * per_owner, (n + 1) * per_owner)
        ref[: per_owner * rows, :] = sums[own.start * rows : own.stop * rows]
        ref[per_owner * rows :, :] = stats_tile([peak[h] for h in own] + [total[h] for h in own], rows)


def attend(bits, rels, limits, q_parts, kv_held):
    rows, key_count = limits.shape[0], kv_held[0].shape[0] // 2
    height = rows * (GROUP >> bits)
    pairs = rows * (GROUP >> bits) * len(rels) * key_count * KVH
    return pl.pallas_call(
        functools.partial(attend_kernel, bits, key_count, rels),
        out_shape=[jax.ShapeDtypeStruct((height + 8, HD), jnp.float32)] * len(rels),
        in_specs=[IN_VMEM] * (1 + len(q_parts) + KVH),
        out_specs=[IN_VMEM] * len(rels),
        compiler_params=limit(16),
        cost_estimate=pl.CostEstimate(
            flops=12 * pairs * HD, bytes_accessed=4 * height * HD, transcendentals=pairs
        ),
        name="attend",
    )(limits, *q_parts, *kv_held)


def merged(parts, heads):
    rows = (parts[0][0].shape[0] - 8) // heads

    def ordered(x, sizes):
        return functools.reduce(swap_rows, sizes, x)

    tiles = [(ref[heads * rows :, :], sizes) for ref, sizes in parts]

    def stat(i):
        return [ordered(stats_column(tile, i, 2 * heads, rows), sizes) for tile, sizes in tiles]

    sums, totals = [], []
    for i in range(heads):
        peaks = stat(i)
        peak = functools.reduce(jnp.maximum, peaks)
        factors = [jnp.exp(x - peak) for x in peaks]
        held = [ordered(ref[i * rows : (i + 1) * rows, :], sizes) for ref, sizes in parts]
        sums.append(sum(x * f for x, f in zip(held, factors)))
        totals.append(sum(x * f for x, f in zip(stat(heads + i), factors)))
    return sums, totals


def project_kernel(swaps, tile, *refs):
    parts, refs = list(zip(refs[: len(swaps)], swaps)), refs[len(swaps) :]
    piece_refs, (send_out, keep_out) = refs[:-2], refs[-2:]
    sums, totals = merged(parts, sum(ref.shape[0] for ref in piece_refs[::2]) // HD)
    attended = jnp.concatenate([a / t for a, t in zip(sums, totals)], axis=1)
    rows = attended.shape[0]
    half = rows // 2
    a1, a2 = pieces_of(attended, 2)
    a12 = jnp.concatenate([a1, a2], axis=0)
    for c in range(keep_out.shape[1] // tile):
        cols = slice(c * tile, (c + 1) * tile)
        out, first = 0.0, 0
        for high_ref, low_ref in zip(piece_refs[::2], piece_refs[1::2]):
            used = slice(first, first + high_ref.shape[0])
            first = used.stop
            top = times(a12[:, used], high_ref[:, cols])
            out = out + (top[:rows] + (top[rows:] + times(a1[:, used], low_ref[:, cols])))
        keep_out[:, cols] = out[:half]
        send_out[:, cols] = out[half:]


def project(swaps, parts, pieces):
    width, heads = pieces[0].shape[1], sum(x.shape[0] for x in pieces[::2]) // HD
    rows = (parts[0].shape[0] - 8) // heads
    out = jax.ShapeDtypeStruct((rows // 2, width), jnp.float32)
    return pl.pallas_call(
        functools.partial(project_kernel, swaps, min(width, 512)),
        out_shape=[out, out],
        in_specs=[IN_VMEM] * (len(parts) + len(pieces)),
        out_specs=[IN_VMEM] * 2,
        compiler_params=limit(16),
        name="project",
    )(*parts, *pieces)


def by_planes(bits, queries, keys, values, weight, lengths):
    blocks = lax.axis_size("blk")
    sub = 1 << bits
    local_rows = queries.shape[0]
    part = KVH * local_rows

    def swap(x, mask):
        return lax.ppermute(x, "blk", [(i, i ^ mask) for i in range(blocks)])

    q_send, limits = pack_q(bits, lengths, queries)
    kv_send = pack_kv(bits, keys, values)
    kv_held = [kv_send[0]] + [swap(kv_send[k], k * sub) for k in range(1, KVH)]
    wide = GROUP * HD
    far = swap(q_send[0], 2 * sub)
    mine = jnp.concatenate([q_send[1], far[:, :wide]], axis=0)
    other = jnp.concatenate([q_send[2], far[:, wide:]], axis=0)
    from_z, from_y = swap(other, sub), swap(mine, 2)
    from_yz = swap(other, 2 + sub)
    q_parts = [jnp.concatenate([mine, from_z], axis=0), jnp.concatenate([from_y, from_yz], axis=0)]
    q_parts = q_parts + [swap(x, 1) for x in q_parts]
    features = weight.shape[0]
    pieces = []
    for i in range(2):
        pieces += split_weight(weight, i * features // 2, features // 2)

    core, side = part << 1, part
    far = attend(bits, (3, 2), limits, q_parts, kv_held)
    near = attend(bits, (1, 0), limits, q_parts, kv_held)
    partials = [near[1], swap(near[0], 1), swap(far[1], 2), swap(far[0], 3)]
    send, keep = project(((), (core,), (side,), (core, side)), partials, pieces)

    recv = swap(send, 1)
    quarter = keep.shape[0] // 4
    rows = [slice(i * quarter, (i + 1) * quarter) for i in range(4)]
    total = keep[rows[0]] + recv[rows[0]]
    for i, mask in ((1, sub), (2, 2), (3, 2 + sub)):
        total = total + swap(keep[rows[i]] + recv[rows[i]], mask)
    out = total[:local_rows] + swap(total[local_rows:], 2 * sub)
    return out


def head_partials(query_rows, keys_held, values_held, key_pos, lengths):
    row_count = query_rows.shape[0]
    grouped = query_rows.reshape(row_count, GROUP, HD)
    scores = jnp.einsum(
        "tje,pe->tjp", grouped, keys_held, precision=HIGHEST, preferred_element_type=jnp.float32
    ) * (1.0 / math.sqrt(HD))
    request_ids = jnp.arange(row_count, dtype=jnp.int32) // REQ_TOK
    request_table = jnp.arange(lengths.shape[0], dtype=jnp.int32)
    limits = jnp.sum(
        jnp.where(request_ids[:, None] == request_table[None, :], lengths[None, :], 0), axis=1
    )
    visible = (key_pos[None, :] < limits[:, None])[:, None, :]
    masked = jnp.where(visible, scores, NEG_FILL)
    peak_vals = jnp.max(masked, axis=2)
    weights = jnp.where(visible, jnp.exp(masked - peak_vals[..., None]), 0.0)
    totals = jnp.sum(weights, axis=2)
    mixed_values = jnp.einsum(
        "tjp,pe->tje", weights, values_held, precision=HIGHEST, preferred_element_type=jnp.float32
    )
    return mixed_values.reshape(row_count, GROUP * HD), peak_vals, totals


def by_all_to_all(queries, keys, values, weight, lengths):
    blocks = lax.axis_size("blk")
    position = lax.axis_index("blk")
    local_rows = queries.shape[0]
    total_rows = local_rows * blocks
    key_count = keys.shape[0]
    sub_count = blocks // KVH
    sub_len = key_count // sub_count

    def exchange(x, split, concat):
        return lax.all_to_all(x, "blk", split_axis=split, concat_axis=concat, tiled=True)

    def spread(x):
        split = x.reshape(sub_count, sub_len, KVH, HD).transpose(0, 2, 1, 3)
        return exchange(split.reshape(blocks, sub_len, HD), 0, 0).reshape(blocks * sub_len, HD)

    held_pos = (
        jnp.arange(blocks, dtype=jnp.int32)[:, None] * key_count
        + position // KVH * sub_len
        + jnp.arange(sub_len, dtype=jnp.int32)[None, :]
    ).reshape(blocks * sub_len)
    query_heads = queries.reshape(local_rows, KVH, GROUP * HD).transpose(1, 0, 2)
    query_send = jnp.broadcast_to(query_heads[None], (sub_count, KVH, local_rows, GROUP * HD))
    query_held = exchange(query_send.reshape(blocks, local_rows, GROUP * HD), 0, 0)
    sums, peaks, totals = head_partials(
        query_held.reshape(total_rows, GROUP * HD), spread(keys), spread(values), held_pos, lengths
    )
    sums = exchange(sums, 0, 0).reshape(sub_count, KVH, local_rows, GROUP, HD)
    peaks = exchange(peaks, 0, 0).reshape(sub_count, KVH, local_rows, GROUP)
    totals = exchange(totals, 0, 0).reshape(sub_count, KVH, local_rows, GROUP)
    factor = jnp.exp(peaks - jnp.max(peaks, axis=0)[None])
    numerator = jnp.sum(sums * factor[..., None], axis=0)
    denominator = jnp.sum(totals * factor, axis=0)
    attended = (numerator / denominator[..., None]).transpose(1, 0, 2, 3).reshape(local_rows, H * HD)
    feature_rows = exchange(attended, 1, 0)
    parts = jnp.dot(feature_rows, weight, precision=HIGHEST, preferred_element_type=jnp.float32)
    return jnp.sum(exchange(parts, 0, 0).reshape(blocks, local_rows, weight.shape[1]), axis=0)


def per_device(queries, prefix_keys, prefix_values, out_weight, lengths):
    blocks = lax.axis_size("blk")
    sub = blocks // KVH
    bits = sub.bit_length() - 1
    fits = (
        blocks == KVH << bits
        and bits == 2
        and PLANE_BITS == 2
        and (KVH * queries.shape[0]) % 8 == 0
        and queries.shape[0] * blocks // 8 * 2 * (GROUP >> bits) <= LANES
        and prefix_keys.shape[0] % LANES == 0
    )
    if fits:
        return by_planes(bits, queries, prefix_keys, prefix_values, out_weight, lengths)
    return by_all_to_all(queries, prefix_keys, prefix_values, out_weight, lengths)


def solution(mesh):
    in_specs = (
        P(("groups", "blk"), None),
        P(("groups", "blk"), None),
        P(("groups", "blk"), None),
        P("blk", None),
        P("groups"),
    )
    out_specs = P(("groups", "blk"), None)
    return jax.shard_map(
        per_device, mesh=mesh, in_specs=in_specs, out_specs=out_specs, check_vma=False
    )
```

```python
import functools
import math

import jax
import jax.numpy as jnp
from jax import lax
from jax.experimental import pallas as pl
from jax.experimental.pallas import tpu as pltpu
from jax.sharding import PartitionSpec as P


H = 64
KVH = 4
HD = 128
REQ_TOK = 16
GROUP = H // KVH
PLANE_BITS = KVH.bit_length() - 1
LANES = 128

HIGHEST = lax.Precision.HIGHEST
NEG_FILL = -1e30


VMEM = pltpu.VMEM


def relative(order, bits):
    out = 0
    for b in range(PLANE_BITS):
        out = out + (((order >> (PLANE_BITS - 1 - b)) & 1) << (bits + b))
    for b in range(bits):
        out = out + (((order >> (PLANE_BITS + bits - 1 - b)) & 1) << b)
    return out


def swap_rows(x, size):
    blocks = [x[i * size : (i + 1) * size] for i in range(x.shape[0] // size)]
    return jnp.concatenate([blocks[i ^ 1] for i in range(len(blocks))], axis=0)


def stats_tile(columns, rows):
    lane = lax.broadcasted_iota(jnp.int32, (8, LANES), 1)
    out = jnp.zeros((8, LANES), jnp.float32)
    for g in range(rows // 8):
        for i, column in enumerate(columns):
            out = jnp.where(lane == g * len(columns) + i, column[8 * g : 8 * g + 8], out)
    return out


def stats_column(tile, i, count, rows):
    return jnp.concatenate([tile[:, g * count + i :][:, :1] for g in range(rows // 8)], axis=0)


def pieces_of(x, count):
    out = []
    for _ in range(count):
        out.append(x.astype(jnp.bfloat16))
        x = x - out[-1].astype(jnp.float32)
    return out


def times(a, b, dims=(((1,), (0,)), ((), ()))):
    return lax.dot_general(a, b, dims, preferred_element_type=jnp.float32)


def limit(mib):
    return pltpu.CompilerParams(vmem_limit_bytes=mib << 20)


IN_VMEM = pl.BlockSpec(memory_space=VMEM)
IN_PLACE = pl.BlockSpec(memory_space=pl.ANY)


def in_hbm(x):
    return pltpu.with_memory_space_constraint(x, pltpu.HBM)


def run_copies(pairs, sems):
    copies = [pltpu.make_async_copy(src, dst, sems.at[i]) for i, (src, dst) in enumerate(pairs)]
    for copy in copies:
        copy.start()
    return copies


def pack_q_kernel(bits, len_hbm, q_hbm, *refs):
    q_outs, (limit_out, len_ref, sems) = refs[:-3], refs[-3:]
    position = lax.axis_index("blk")
    wide, half = GROUP * HD, KVH // 2
    pairs = [(len_hbm, len_ref)]
    for step in reversed(range(KVH)):
        lanes = pl.ds(pl.multiple_of(((position >> bits) ^ step) * wide, wide), wide)
        q_out = q_outs[0].at[:, pl.ds((step - half) * wide, wide)] if step >= half else q_outs[1 + step]
        pairs.append((q_hbm.at[:, lanes], q_out))
    copies = run_copies(pairs, sems)
    local_rows = q_hbm.shape[0]
    row = lax.broadcasted_iota(jnp.int32, limit_out.shape, 0)
    token = (position ^ relative(row // local_rows, bits)) * local_rows + row % local_rows
    request = token // REQ_TOK
    copies[0].wait()
    limits = jnp.zeros(limit_out.shape, jnp.int32)
    for i in range(len_ref.shape[0]):
        limits = jnp.where(request == i, len_ref[i], limits)
    limit_out[...] = limits
    for copy in copies[1:]:
        copy.wait()


def pack_q(bits, lengths, queries):
    local_rows, wide = queries.shape[0], GROUP * HD
    q_high = jax.ShapeDtypeStruct((local_rows, KVH // 2 * wide), jnp.float32)
    q = jax.ShapeDtypeStruct((local_rows, wide), jnp.float32)
    limits = jax.ShapeDtypeStruct(((KVH << bits) * local_rows, LANES), jnp.int32)
    out = pl.pallas_call(
        functools.partial(pack_q_kernel, bits),
        out_shape=[q_high] + [q] * (KVH // 2) + [limits],
        in_specs=[IN_PLACE] * 2,
        out_specs=[IN_VMEM] * (KVH // 2 + 2),
        scratch_shapes=[pltpu.SMEM(lengths.shape, jnp.int32), pltpu.SemaphoreType.DMA((1 + KVH,))],
        compiler_params=limit(4),
        name="pack_q",
    )(in_hbm(lengths), in_hbm(queries))
    return out[:-1], out[-1]


def pack_kv_kernel(bits, k_hbm, v_hbm, *refs):
    kv_outs, sems = refs[:-1], refs[-1]
    plane = lax.axis_index("blk") >> bits
    keys = k_hbm.shape[0]
    pairs = []
    for step in reversed(range(KVH)):
        lanes = pl.ds(pl.multiple_of((plane ^ step) * HD, HD), HD)
        pairs.append((k_hbm.at[:, lanes], kv_outs[step].at[pl.ds(0, keys), :]))
        pairs.append((v_hbm.at[:, lanes], kv_outs[step].at[pl.ds(keys, keys), :]))
    for copy in run_copies(pairs, sems):
        copy.wait()


def pack_kv(bits, keys, values):
    kv = jax.ShapeDtypeStruct((2 * keys.shape[0], HD), jnp.float32)
    return pl.pallas_call(
        functools.partial(pack_kv_kernel, bits),
        out_shape=[kv] * KVH,
        in_specs=[IN_PLACE] * 2,
        out_specs=[IN_VMEM] * KVH,
        scratch_shapes=[pltpu.SemaphoreType.DMA((2 * KVH,))],
        compiler_params=limit(4),
        cost_estimate=pl.CostEstimate(flops=0, bytes_accessed=16 * keys.size, transcendentals=0),
        name="pack_kv",
    )(in_hbm(keys), in_hbm(values))


def split_kernel(first, tile, w_hbm, high_ref, low_ref, buf, sems):
    chunks = buf.shape[0]
    copies = [
        pltpu.make_async_copy(w_hbm.at[pl.ds(first + c * tile, tile), :], buf.at[c], sems.at[c])
        for c in range(chunks)
    ]
    for copy in copies:
        copy.start()
    for c in range(chunks):
        copies[c].wait()
        rows = slice(c * tile, (c + 1) * tile)
        high_ref[rows, :], low_ref[rows, :] = pieces_of(buf[c], 2)


def split_weight(weight, first, count):
    width = weight.shape[1]
    tile = min(count, 64)
    out = jax.ShapeDtypeStruct((count, width), jnp.bfloat16)
    return pl.pallas_call(
        functools.partial(split_kernel, first, tile),
        out_shape=[out, out],
        in_specs=[IN_PLACE],
        out_specs=[IN_VMEM] * 2,
        scratch_shapes=[
            pltpu.VMEM((count // tile, tile, width), jnp.float32),
            pltpu.SemaphoreType.DMA((count // tile,)),
        ],
        compiler_params=limit(12),
        cost_estimate=pl.CostEstimate(
            flops=8 * count * width, bytes_accessed=8 * count * width, transcendentals=0
        ),
        name="split",
    )(in_hbm(weight))


def attend_kernel(bits, key_count, rels, limit_ref, *refs):
    sub = 1 << bits
    inputs, outs = refs[: -len(rels)], refs[-len(rels) :]
    q_refs, kv_refs = inputs[:-KVH], inputs[-KVH:]
    position = lax.axis_index("blk")
    plane, place = position // sub, position % sub
    rows = limit_ref.shape[0]
    per_owner = GROUP // sub
    held = key_count * KVH

    at = lax.broadcasted_iota(jnp.int32, (1, held), 1)
    source = (plane ^ (at // key_count)) * sub + place
    visible = (source * key_count + at % key_count) < limit_ref[:, :1]

    keys = jnp.concatenate([r[:key_count, :] for r in kv_refs], axis=0)
    values = jnp.concatenate([r[key_count:, :] for r in kv_refs], axis=0)
    k1, k2, k3 = pieces_of(keys, 3)
    k12, k31 = jnp.concatenate([k1, k2], axis=1), jnp.concatenate([k3, k1], axis=1)
    v1, v2 = pieces_of(values, 2)
    v12 = jnp.concatenate([v1, v2], axis=1)
    both = (((1,), (1,)), ((), ()))
    scale = 1.0 / math.sqrt(HD)

    count = len(rels) * per_owner
    cross = jnp.broadcast_to(visible[None], (count, rows, held))
    heads = []
    for rel in rels:
        for i in range(per_owner):
            lanes = pl.ds(pl.multiple_of(((place ^ rel) * per_owner + i) * HD, HD), HD)
            heads += [q_ref[:, lanes] for q_ref in q_refs]
    q1, q2, q3 = pieces_of(jnp.concatenate(heads, axis=0) * scale, 3)
    q11, q22 = jnp.concatenate([q1, q1], axis=1), jnp.concatenate([q2, q2], axis=1)
    q13 = jnp.concatenate([q1, q3], axis=1)
    scores = times(q11, k12, both) + (times(q22, k12, both) + times(q13, k31, both))
    scores = scores.reshape(count, rows, held)
    masked = jnp.where(cross, scores, NEG_FILL)
    peak = jnp.max(masked, axis=2, keepdims=True)
    weights = jnp.where(cross, jnp.exp(masked - peak), 0.0)
    total = jnp.sum(weights, axis=2, keepdims=True)
    w1, w2 = pieces_of(weights.reshape(count * rows, held), 2)
    wide = times(w1, v12)
    sums = wide[:, :HD] + (wide[:, HD:] + times(w2, v1))
    for n, ref in enumerate(outs):
        own = range(n * per_owner, (n + 1) * per_owner)
        ref[: per_owner * rows, :] = sums[own.start * rows : own.stop * rows]
        ref[per_owner * rows :, :] = stats_tile([peak[h] for h in own] + [total[h] for h in own], rows)


def attend(bits, rels, limits, q_parts, kv_held):
    rows, key_count = limits.shape[0], kv_held[0].shape[0] // 2
    height = rows * (GROUP >> bits)
    pairs = rows * (GROUP >> bits) * len(rels) * key_count * KVH
    return pl.pallas_call(
        functools.partial(attend_kernel, bits, key_count, rels),
        out_shape=[jax.ShapeDtypeStruct((height + 8, HD), jnp.float32)] * len(rels),
        in_specs=[IN_VMEM] * (1 + len(q_parts) + KVH),
        out_specs=[IN_VMEM] * len(rels),
        compiler_params=limit(16),
        cost_estimate=pl.CostEstimate(
            flops=12 * pairs * HD, bytes_accessed=4 * height * HD, transcendentals=pairs
        ),
        name="attend",
    )(limits, *q_parts, *kv_held)


def merged(parts, heads):
    rows = (parts[0][0].shape[0] - 8) // heads

    def ordered(x, sizes):
        return functools.reduce(swap_rows, sizes, x)

    tiles = [(ref[heads * rows :, :], sizes) for ref, sizes in parts]

    def stat(i):
        return [ordered(stats_column(tile, i, 2 * heads, rows), sizes) for tile, sizes in tiles]

    sums, totals = [], []
    for i in range(heads):
        peaks = stat(i)
        peak = functools.reduce(jnp.maximum, peaks)
        factors = [jnp.exp(x - peak) for x in peaks]
        held = [ordered(ref[i * rows : (i + 1) * rows, :], sizes) for ref, sizes in parts]
        sums.append(sum(x * f for x, f in zip(held, factors)))
        totals.append(sum(x * f for x, f in zip(stat(heads + i), factors)))
    return sums, totals


def project_kernel(swaps, tile, *refs):
    parts, refs = list(zip(refs[: len(swaps)], swaps)), refs[len(swaps) :]
    piece_refs, (send_out, keep_out) = refs[:-2], refs[-2:]
    sums, totals = merged(parts, sum(ref.shape[0] for ref in piece_refs[::2]) // HD)
    attended = jnp.concatenate([a / t for a, t in zip(sums, totals)], axis=1)
    rows = attended.shape[0]
    half = rows // 2
    a1, a2 = pieces_of(attended, 2)
    a12 = jnp.concatenate([a1, a2], axis=0)
    for c in range(keep_out.shape[1] // tile):
        cols = slice(c * tile, (c + 1) * tile)
        out, first = 0.0, 0
        for high_ref, low_ref in zip(piece_refs[::2], piece_refs[1::2]):
            used = slice(first, first + high_ref.shape[0])
            first = used.stop
            top = times(a12[:, used], high_ref[:, cols])
            out = out + (top[:rows] + (top[rows:] + times(a1[:, used], low_ref[:, cols])))
        keep_out[:, cols] = out[:half]
        send_out[:, cols] = out[half:]


def project(swaps, parts, pieces):
    width, heads = pieces[0].shape[1], sum(x.shape[0] for x in pieces[::2]) // HD
    rows = (parts[0].shape[0] - 8) // heads
    out = jax.ShapeDtypeStruct((rows // 2, width), jnp.float32)
    return pl.pallas_call(
        functools.partial(project_kernel, swaps, min(width, 512)),
        out_shape=[out, out],
        in_specs=[IN_VMEM] * (len(parts) + len(pieces)),
        out_specs=[IN_VMEM] * 2,
        compiler_params=limit(16),
        name="project",
    )(*parts, *pieces)


def by_planes(bits, queries, keys, values, weight, lengths):
    blocks = lax.axis_size("blk")
    sub = 1 << bits
    local_rows = queries.shape[0]
    part = KVH * local_rows

    def swap(x, mask):
        return lax.ppermute(x, "blk", [(i, i ^ mask) for i in range(blocks)])

    q_send, limits = pack_q(bits, lengths, queries)
    kv_send = pack_kv(bits, keys, values)
    kv_held = [kv_send[0]] + [swap(kv_send[k], k * sub) for k in range(1, KVH)]
    wide = GROUP * HD
    q_rows = [[q] for q in q_send[1:]]
    q_out = q_send[0]
    for b in reversed(range(PLANE_BITS)):
        q_in = swap(q_out, sub << b)
        count = len(q_rows[0])
        got = [q_in[:, i * wide : (i + 1) * wide] for i in range(q_in.shape[1] // wide)]
        q_rows = [rows + got[t * count : (t + 1) * count] for t, rows in enumerate(q_rows)]
        high = q_rows[len(q_rows) // 2 :]
        if b:
            q_out = jnp.concatenate([piece for rows in high for piece in rows], axis=1)
            q_rows = q_rows[: len(q_rows) // 2]
    q_parts = [jnp.concatenate(q_rows[0], axis=0)]
    for b in reversed(range(bits)):
        q_parts = q_parts + [swap(x, 1 << b) for x in q_parts]
    features = weight.shape[0]
    pieces = []
    for i in range(2):
        pieces += split_weight(weight, i * features // 2, features // 2)

    core, side = part << 1, part
    far = attend(bits, (3, 2), limits, q_parts, kv_held)
    near = attend(bits, (1, 0), limits, q_parts, kv_held)
    partials = [near[1], swap(near[0], 1), swap(far[1], 2), swap(far[0], 3)]
    send, keep = project(((), (core,), (side,), (core, side)), partials, pieces)

    recv = swap(send, 1)
    quarter = keep.shape[0] // 4
    rows = [slice(i * quarter, (i + 1) * quarter) for i in range(4)]
    total = keep[rows[0]] + recv[rows[0]]
    for i, mask in ((1, sub), (2, 2), (3, 2 + sub)):
        total = total + swap(keep[rows[i]] + recv[rows[i]], mask)
    out = total[:local_rows] + swap(total[local_rows:], 2 * sub)
    return out


def head_partials(query_rows, keys_held, values_held, key_pos, lengths):
    row_count = query_rows.shape[0]
    grouped = query_rows.reshape(row_count, GROUP, HD)
    scores = jnp.einsum(
        "tje,pe->tjp", grouped, keys_held, precision=HIGHEST, preferred_element_type=jnp.float32
    ) * (1.0 / math.sqrt(HD))
    request_ids = jnp.arange(row_count, dtype=jnp.int32) // REQ_TOK
    request_table = jnp.arange(lengths.shape[0], dtype=jnp.int32)
    limits = jnp.sum(
        jnp.where(request_ids[:, None] == request_table[None, :], lengths[None, :], 0), axis=1
    )
    visible = (key_pos[None, :] < limits[:, None])[:, None, :]
    masked = jnp.where(visible, scores, NEG_FILL)
    peak_vals = jnp.max(masked, axis=2)
    weights = jnp.where(visible, jnp.exp(masked - peak_vals[..., None]), 0.0)
    totals = jnp.sum(weights, axis=2)
    mixed_values = jnp.einsum(
        "tjp,pe->tje", weights, values_held, precision=HIGHEST, preferred_element_type=jnp.float32
    )
    return mixed_values.reshape(row_count, GROUP * HD), peak_vals, totals


def by_all_to_all(queries, keys, values, weight, lengths):
    blocks = lax.axis_size("blk")
    position = lax.axis_index("blk")
    local_rows = queries.shape[0]
    total_rows = local_rows * blocks
    key_count = keys.shape[0]
    sub_count = blocks // KVH
    sub_len = key_count // sub_count

    def exchange(x, split, concat):
        return lax.all_to_all(x, "blk", split_axis=split, concat_axis=concat, tiled=True)

    def spread(x):
        split = x.reshape(sub_count, sub_len, KVH, HD).transpose(0, 2, 1, 3)
        return exchange(split.reshape(blocks, sub_len, HD), 0, 0).reshape(blocks * sub_len, HD)

    held_pos = (
        jnp.arange(blocks, dtype=jnp.int32)[:, None] * key_count
        + position // KVH * sub_len
        + jnp.arange(sub_len, dtype=jnp.int32)[None, :]
    ).reshape(blocks * sub_len)
    query_heads = queries.reshape(local_rows, KVH, GROUP * HD).transpose(1, 0, 2)
    query_send = jnp.broadcast_to(query_heads[None], (sub_count, KVH, local_rows, GROUP * HD))
    query_held = exchange(query_send.reshape(blocks, local_rows, GROUP * HD), 0, 0)
    sums, peaks, totals = head_partials(
        query_held.reshape(total_rows, GROUP * HD), spread(keys), spread(values), held_pos, lengths
    )
    sums = exchange(sums, 0, 0).reshape(sub_count, KVH, local_rows, GROUP, HD)
    peaks = exchange(peaks, 0, 0).reshape(sub_count, KVH, local_rows, GROUP)
    totals = exchange(totals, 0, 0).reshape(sub_count, KVH, local_rows, GROUP)
    factor = jnp.exp(peaks - jnp.max(peaks, axis=0)[None])
    numerator = jnp.sum(sums * factor[..., None], axis=0)
    denominator = jnp.sum(totals * factor, axis=0)
    attended = (numerator / denominator[..., None]).transpose(1, 0, 2, 3).reshape(local_rows, H * HD)
    feature_rows = exchange(attended, 1, 0)
    parts = jnp.dot(feature_rows, weight, precision=HIGHEST, preferred_element_type=jnp.float32)
    return jnp.sum(exchange(parts, 0, 0).reshape(blocks, local_rows, weight.shape[1]), axis=0)


def per_device(queries, prefix_keys, prefix_values, out_weight, lengths):
    blocks = lax.axis_size("blk")
    sub = blocks // KVH
    bits = sub.bit_length() - 1
    fits = (
        blocks == KVH << bits
        and bits == 2
        and PLANE_BITS == 2
        and (KVH * queries.shape[0]) % 8 == 0
        and queries.shape[0] * blocks // 8 * 2 * (GROUP >> bits) <= LANES
        and prefix_keys.shape[0] % LANES == 0
    )
    if fits:
        return by_planes(bits, queries, prefix_keys, prefix_values, out_weight, lengths)
    return by_all_to_all(queries, prefix_keys, prefix_values, out_weight, lengths)


def solution(mesh):
    in_specs = (
        P(("groups", "blk"), None),
        P(("groups", "blk"), None),
        P(("groups", "blk"), None),
        P("blk", None),
        P("groups"),
    )
    out_specs = P(("groups", "blk"), None)
    return jax.shard_map(
        per_device, mesh=mesh, in_specs=in_specs, out_specs=out_specs, check_vma=False
    )
```
